512 devices in a mesh: section: 8 (over z), dp: 32 (over y_lo, x, core), seq: 2 (over y_hi).
Axes of the slice: x: 4, y: 8 (y_hi: 2, y_lo: 4; y = y_hi * 4 + y_lo), z: 8, core: 2. Of those that a mesh axis runs over, the one named last changes fastest.
Arguments:
- section_input: bfloat16 [8, 2048, 5120], P('section', 'seq', 'dp'), as said below
- norm_gain: bfloat16 [8, 5120], P('section', 'dp'), may hold values from 0.5 to 2
- qkv_weight: bfloat16 [8, 5120, 12288], P('section', 'seq', 'dp'), as said below
- out_weight: bfloat16 [8, 4096, 5120], P('section', None, 'dp'), may hold values from -0.5 to 0.5
- random_blocks: int32 [8, 32, 3], P('section', 'seq'), may hold values from 0 to 31
- global_blocks: int32 [8, 2], P('section'), may hold values from 0 to 31, as said below
Outputs:
- handed_on: bfloat16 [8, 2048, 5120], P('section', 'seq', 'dp')
The draws below stay inside these ranges and needn't reach their ends.
Inputs may be any that keep to these rules, and one draw needn't show every extreme that they name: `section_input`: real values, each token row and each feature column with its own scale. `qkv_weight`: real values of projections. `global_blocks`: 2 different block numbers for each section; the last section's document has the first and the last block as its global blocks.
All inputs are finite; a program needn't handle non-finite values.
Results may differ from the reference program's by a relative error of at most 0.0058.
Values may be sent and summed in bfloat16 or wider, within the bound.
No kernel may reach another device: no remote copies, remote signals or barrier semaphores. Data moves between devices by JAX's collectives and lax.ppermute only.
A program may use at most 64 MiB of HBM per device.

```python
import math
import jax
import jax.numpy as jnp
from jax import lax

D = 5120
HD = 128
BLOCK = 64
RANDOMS = 3
GLOBALS = 2
TOKENS = 2048
NB = 32
HEADS = 32
SECTIONS = 8


def draw_section_input(key, part):
    base_key, row_key, col_key = jax.random.split(key, 3)
    base = jnp.clip(jax.random.normal(base_key, (SECTIONS, TOKENS, D), jnp.float32), -6.0, 6.0)
    row_scale = jnp.exp(jax.random.uniform(row_key, (SECTIONS, TOKENS, 1), jnp.float32, math.log(0.3), math.log(3.0)))
    col_scale = jnp.exp(jax.random.uniform(col_key, (SECTIONS, 1, D), jnp.float32, math.log(0.4), math.log(4.0)))
    position = jnp.arange(D, dtype=jnp.float32) / (D - 1)
    ramp = jnp.exp(0.5 * math.log(3.0) * position)
    values = base * row_scale * col_scale * ramp[None, None, :]
    return values.astype(jnp.bfloat16)


def draw_qkv_weight(key, part):
    raw_key = jax.random.fold_in(key, 0)
    raw = jnp.clip(jax.random.normal(raw_key, (SECTIONS, D, HEADS, 3, HD), jnp.float32), -6.0, 6.0)
    factor = jnp.array([1.2, 1.2, 1.0], jnp.float32)[None, None, None, :, None]
    full = raw * factor / math.sqrt(D)
    return full.reshape(SECTIONS, D, HEADS * 3 * HD).astype(jnp.bfloat16)


def draw_global_blocks(key, part):
    section_keys = jax.random.split(jax.random.fold_in(key, 17), SECTIONS)

    def pick(one_key):
        return jax.random.permutation(one_key, NB)[:GLOBALS].astype(jnp.int32)
    picked = jax.vmap(pick)(section_keys)
    ends = jnp.zeros((GLOBALS,), jnp.int32).at[GLOBALS - 1].set(NB - 1)
    is_last = (jnp.arange(SECTIONS, dtype=jnp.int32) == SECTIONS - 1)[:, None]
    return jnp.where(is_last, ends[None, :], picked).astype(jnp.int32)


def place_ends(entries, stream_key, low, top_value):
    extent = entries.shape
    spot = [jax.random.randint(jax.random.fold_in(stream_key, axis), (), 0, extent[axis]) for axis in range(len(extent))]
    entries = entries.at[tuple(spot)].set(low)
    longest = extent.index(max(extent))
    spot[longest] = (spot[longest] + 1) % extent[longest]
    return entries.at[tuple(spot)].set(top_value)


def level_of(key, dims, shards, low, top_value):
    level, own = 1.0, jax.random.fold_in(key, 6)
    for axis_at, parts in shards:
        heights = jnp.exp(jax.random.uniform(jax.random.fold_in(own, axis_at), (parts,), jnp.float32, low / len(shards), top_value / len(shards)))
        level = level * jnp.repeat(heights, dims[axis_at] // parts).reshape([-1 if axis == axis_at else 1 for axis in range(len(dims))])
    return level


def bell_draw(key, dims, deviation, bound, cuts=(), held_as=jnp.bfloat16):
    drawn = deviation * jax.random.normal(key, dims, jnp.float32)
    if cuts:
        drawn = drawn * level_of(key, dims, cuts, -0.22, 0.18)
    return jnp.clip(drawn, -bound, bound).astype(held_as)


def setup_inputs(seed: int = 0) -> dict:
    key_list = jax.random.split(jax.random.key(seed), 7)
    section_input = draw_section_input(jax.random.fold_in(key_list[6], 71), 0)
    norm_gain = jnp.clip(jnp.exp(math.log(2.0) - 1.3862944 * jax.random.uniform(key_list[1], (SECTIONS, D), jnp.float32) ** level_of(key_list[1], (SECTIONS, D), ((0, 8), (1, 32)), -0.2, 0.2)), 0.5, 2.0).astype(jnp.bfloat16)
    qkv_weight = draw_qkv_weight(jax.random.fold_in(key_list[6], 71), 0)
    out_weight = bell_draw(key_list[3], (SECTIONS, HEADS * HD, D), (HEADS * HD // 32) ** -0.5, 0.5, ((0, 8), (2, 32)))
    random_blocks = place_ends(jax.random.randint(key_list[4], (SECTIONS, NB, RANDOMS), 0, NB), jax.random.fold_in(key_list[4], 1), 0, NB - 1).astype(jnp.int32)
    global_blocks = draw_global_blocks(jax.random.fold_in(key_list[6], 71), 0)
    return {"section_input": section_input, "norm_gain": norm_gain, "qkv_weight": qkv_weight, "out_weight": out_weight, "random_blocks": random_blocks, "global_blocks": global_blocks}


def block_mask(query_ids, random_rows, global_ids, key_count):
    query_col = query_ids[:, None]
    key_ids = jnp.arange(key_count, dtype=jnp.int32)[None, :]
    adjacent = jnp.abs(query_col - key_ids) <= 1
    key_global = jnp.any(key_ids[:, :, None] == global_ids[None, None, :], axis=2)
    query_global = jnp.any(query_col[:, :, None] == global_ids[None, None, :], axis=2)
    chosen = jnp.any(random_rows[:, None, :] == key_ids[:, :, None], axis=2)
    return adjacent | key_global | query_global | chosen

def sparse_attention(query, keys, values, allowed, block_size):
    scores = lax.dot_general(query, keys, (((1,), (1,)), ((), ())), preferred_element_type=jnp.float32)
    scores = scores * (1.0 / math.sqrt(query.shape[1]))
    query_blocks, key_blocks = allowed.shape
    scores = scores.reshape(query_blocks, block_size, key_blocks, block_size)
    live = allowed[:, None, :, None]
    scores = jnp.where(live, scores, -1e+30)
    highest = lax.optimization_barrier(jnp.max(scores, axis=(2, 3), keepdims=True))
    weights = jnp.where(live, jnp.exp(scores - highest), 0.0)
    totals = lax.optimization_barrier(jnp.sum(weights, axis=(2, 3), keepdims=True))
    probs = (weights / totals).reshape(query_blocks * block_size, key_blocks * block_size).astype(jnp.bfloat16)
    return jnp.dot(probs, values, preferred_element_type=jnp.float32).astype(jnp.bfloat16)

def section_layer(activations, gain, projection, out_proj, random_rows, global_ids):
    length = activations.shape[0]
    as_float = activations.astype(jnp.float32)
    mean_sq = lax.optimization_barrier(jnp.mean(as_float * as_float, axis=1, keepdims=True))
    normed = (as_float * lax.rsqrt(mean_sq + 1e-05) * gain.astype(jnp.float32)).astype(jnp.bfloat16)
    joined = jnp.dot(normed, projection, preferred_element_type=jnp.float32)
    count = length // BLOCK
    allowed = block_mask(jnp.arange(count, dtype=jnp.int32), random_rows, global_ids, count)
    pieces = joined.reshape(length, HEADS, 3, HD).astype(jnp.bfloat16)
    pieces = jnp.transpose(pieces, (1, 2, 0, 3))

    def one_head(item):
        return sparse_attention(item[0], item[1], item[2], allowed, BLOCK)
    head_results = lax.map(one_head, pieces)
    attended = jnp.transpose(head_results, (1, 0, 2)).reshape(length, HEADS * HD)
    added = jnp.dot(attended, out_proj, preferred_element_type=jnp.float32)
    return (as_float + added).astype(jnp.bfloat16)

def reference(section_input, norm_gain, qkv_weight, out_weight, random_blocks, global_blocks):
    results = []
    for section_index in range(SECTIONS):
        results.append(section_layer(section_input[section_index], norm_gain[section_index], qkv_weight[section_index], out_weight[section_index], random_blocks[section_index], global_blocks[section_index]))
    return jnp.roll(jnp.stack(results), 1, axis=0)
```

```python
import math

import jax
import jax.numpy as jnp
from jax import lax
from jax.experimental import pallas as pl
from jax.experimental.pallas import tpu as pltpu
from jax.sharding import Mesh, PartitionSpec as P

BLOCK = 64
CHUNKS = 2
PLANE = ("yl", "x", "core", "seq")
DP = ("yl", "x", "core")
NEG = -1e30


def moved(value, where):
    pairs = []
    for yl in range(4):
        for x in range(4):
            for core in range(2):
                for seq in range(2):
                    target = where(seq * 4 + yl, x, core)
                    if target is None:
                        continue
                    ty, tx, tc = target
                    source_at = ((yl * 4 + x) * 2 + core) * 2 + seq
                    target_at = (((ty % 4) * 4 + tx) * 2 + tc) * 2 + ty // 4
                    pairs.append((source_at, target_at))
    return lax.ppermute(value, PLANE, pairs)


def swap_inner(y, x, core):
    if y in (2, 3):
        return y + 2, x, core
    if y in (4, 5):
        return y - 2, x, core
    return y, x, core


def sums_over_dp(value):
    for where in (
        lambda y, x, c: (y, x, 1 - c),
        lambda y, x, c: (y, x ^ 1, c),
        lambda y, x, c: (y, x ^ 2, c),
        lambda y, x, c: (y ^ 1, x, c),
        lambda y, x, c: (y ^ 2, x, c),
    ):
        value = value + moved(value, where)
    return value


def other_seq(y, x, core):
    return (y + 4) % 8, x, core


def block_mask(query_ids, random_rows, global_ids, key_count):
    query_col = query_ids[:, None]
    key_ids = jnp.arange(key_count, dtype=jnp.int32)[None, :]
    adjacent = jnp.abs(query_col - key_ids) <= 1
    key_global = jnp.any(key_ids[:, :, None] == global_ids[None, None, :], axis=2)
    query_global = jnp.any(query_col[:, :, None] == global_ids[None, None, :], axis=2)
    chosen = jnp.any(random_rows[:, None, :] == key_ids[:, :, None], axis=2)
    return adjacent | key_global | query_global | chosen


def attention_kernel(scale, query_ref, key_ref, value_ref, live_ref, out_ref, rows_ref):
    @pl.when(pl.program_id(0) == 0)
    def _():
        rows_ref[...] = key_ref[...].T

    scores = jnp.dot(rows_ref[...], query_ref[...], preferred_element_type=jnp.float32)
    keys, queries = scores.shape
    live = jnp.broadcast_to(live_ref[...][:, None, :] > 0, (keys // BLOCK, BLOCK, queries))
    scores = scores.reshape(keys // BLOCK, BLOCK, queries)
    scores = jnp.where(live, scores, NEG)
    highest = jnp.max(scores, axis=(0, 1), keepdims=True)
    weights = jnp.where(live, jnp.exp((scores - highest) * scale), 0.0)
    totals = jnp.sum(weights, axis=(0, 1), keepdims=True)[0]
    weights = weights.reshape(keys, queries).astype(jnp.bfloat16)
    mixed = jnp.dot(value_ref[...], weights, preferred_element_type=jnp.float32)
    out_ref[...] = (mixed / totals).astype(jnp.bfloat16)


def attention(query, key, value, live):
    size, count = query.shape
    tile = 128
    whole = pl.BlockSpec(key.shape, lambda i: (0, 0))
    return pl.pallas_call(
        lambda *refs: attention_kernel(1.0 / math.sqrt(size), *refs),
        grid=(count // tile,),
        in_specs=[
            pl.BlockSpec((size, tile), lambda i: (0, i)),
            whole,
            whole,
            pl.BlockSpec((live.shape[0], tile), lambda i: (0, i)),
        ],
        out_specs=pl.BlockSpec((size, tile), lambda i: (0, i)),
        out_shape=jax.ShapeDtypeStruct(query.shape, jnp.bfloat16),
        scratch_shapes=[pltpu.VMEM((key.shape[1], size), jnp.bfloat16)],
        name="attention",
    )(query, key, value, live)


def shards(section_input, norm_gain, qkv_weight, out_weight, random_blocks, global_blocks):
    seq, core = lax.axis_index("seq"), lax.axis_index("core")
    tokens_t = section_input[0].T
    part, length = tokens_t.shape
    devices = 32
    width = part * devices
    step = length // CHUNKS

    gathered = []
    for j in range(CHUNKS):
        piece = moved(tokens_t[:, j * step : (j + 1) * step], swap_inner)
        piece = lax.all_gather(piece, DP, axis=0, tiled=True)
        gathered.append(piece.reshape(2, width // 2, step))

    as_float = tokens_t.astype(jnp.float32)
    squares = jnp.sum(as_float * as_float, axis=0).reshape(length // 256, 256)
    slot = (lax.axis_index(DP) == jnp.arange(devices))[:, None]
    gains = jnp.where(slot, norm_gain.astype(jnp.float32), 0.0)
    gains = jnp.pad(gains, ((0, 0), (0, 256 - part)))
    both = sums_over_dp(jnp.concatenate([gains, squares], axis=0))
    mine = both[devices:]
    theirs = moved(mine, other_seq)
    squares = jnp.where(seq == 0, jnp.stack([mine, theirs]), jnp.stack([theirs, mine]))
    factor = lax.rsqrt(squares.reshape(2, length) / width + 1e-05)
    gain = lax.dynamic_slice_in_dim(both[:devices, :part], seq * (devices // 2), devices // 2, axis=0)
    gain = gain.reshape(width // 2, 1)

    other_rows = moved(random_blocks[0], other_seq)
    rows = jnp.where(core == seq, random_blocks[0], other_rows)
    own_blocks = length // BLOCK
    query_ids = core * own_blocks + jnp.arange(own_blocks, dtype=jnp.int32)
    allowed = block_mask(query_ids, rows, global_blocks[0], 2 * own_blocks)
    live = jnp.repeat(allowed.T.astype(jnp.float32), BLOCK, axis=1)

    weight_t = qkv_weight[0].T
    head = weight_t.shape[0] // 3
    totals = []
    for j in range(CHUNKS):
        partial = []
        for t in range(2):
            scale = factor[t, j * step : (j + 1) * step]
            normed = gathered[j][t].astype(jnp.float32) * scale[None, :] * gain
            normed = normed.astype(jnp.bfloat16)
            partial.append(jnp.dot(weight_t, normed, preferred_element_type=jnp.float32))
        partial = jnp.stack(partial, axis=1)
        came = moved(
            partial.astype(jnp.bfloat16),
            lambda y, x, c: ((y + 4) % 8, x, c) if c != y // 4 else None,
        )
        totals.append((partial + came.astype(jnp.float32)).astype(jnp.bfloat16))
    joined = jnp.stack(totals, axis=2).reshape(3 * head, 2 * length)
    beside = moved(joined, lambda y, x, c: (y, x, 1 - c) if c == y // 4 else None)
    joined = jnp.where(core == seq, joined, beside)

    query = lax.dynamic_slice_in_dim(joined[:head], core * length, length, axis=1)
    attended = attention(query, joined[head : 2 * head], joined[2 * head :], live)
    def cross(y, x, c):
        return (y, x, c) if c == y // 4 else ((y + 4) % 8, x, 1 - c)

    attended = moved(attended, cross)
    heads = lax.all_gather(attended, DP, axis=0, tiled=True)
    added = jnp.dot(out_weight[0].T, heads, preferred_element_type=jnp.float32)
    result = (as_float + added).astype(jnp.bfloat16)
    sections = lax.axis_size("section")
    route = [((i - 1) % sections, i) for i in range(sections)]
    return lax.ppermute(result.T[None], "section", route)


def solution(mesh):
    fine = Mesh(mesh.devices.reshape(8, 4, 4, 2, 2), ("section", "yl", "x", "core", "seq"))
    placed = (
        P("section", "seq", DP),
        P("section", DP),
        P("section", "seq", DP),
        P("section", None, DP),
        P("section", "seq", None),
        P("section", None),
    )
    return jax.shard_map(
        shards, mesh=fine, in_specs=placed, out_specs=P("section", "seq", DP), check_vma=False
    )
```

```python
import math

import jax
import jax.numpy as jnp
from jax import lax
from jax.experimental import pallas as pl
from jax.experimental.pallas import tpu as pltpu
from jax.sharding import Mesh, PartitionSpec as P

BLOCK = 64
PLANE = ("yl", "x", "core", "seq")
DP = ("yl", "x", "core")
NEG = -1e30


def moved(value, where):
    pairs = []
    for yl in range(4):
        for x in range(4):
            for core in range(2):
                for seq in range(2):
                    target = where(seq * 4 + yl, x, core)
                    if target is None:
                        continue
                    ty, tx, tc = target
                    source_at = ((yl * 4 + x) * 2 + core) * 2 + seq
                    target_at = (((ty % 4) * 4 + tx) * 2 + tc) * 2 + ty // 4
                    pairs.append((source_at, target_at))
    return lax.ppermute(value, PLANE, pairs)


def swap_inner(y, x, core):
    if y in (2, 3):
        return y + 2, x, core
    if y in (4, 5):
        return y - 2, x, core
    return y, x, core


def other_seq(y, x, core):
    return (y + 4) % 8, x, core


def block_mask(query_ids, random_rows, global_ids, key_ids):
    query_col = query_ids[:, None]
    key_ids = key_ids[None, :]
    adjacent = jnp.abs(query_col - key_ids) <= 1
    key_global = jnp.any(key_ids[:, :, None] == global_ids[None, None, :], axis=2)
    query_global = jnp.any(query_col[:, :, None] == global_ids[None, None, :], axis=2)
    chosen = jnp.any(random_rows[:, None, :] == key_ids[:, :, None], axis=2)
    return adjacent | key_global | query_global | chosen


def attention_kernel(scale, own_ref, other_ref, live_ref, out_ref, rows_ref, value_ref):
    size = rows_ref.shape[1]

    @pl.when(pl.program_id(0) == 0)
    def _():
        step = own_ref.shape[2]
        for i in range(2):
            here, there = pl.ds(i * step, step), pl.ds((2 + i) * step, step)
            rows_ref[here, :] = own_ref[i, size : 2 * size, :].T
            rows_ref[there, :] = other_ref[i, :size, :].T
            value_ref[:, here] = own_ref[i, 2 * size :, :]
            value_ref[:, there] = other_ref[i, size:, :]

    tile = out_ref.shape[2]
    per = own_ref.shape[2] // tile
    at = pl.program_id(0)
    columns = pl.ds(pl.multiple_of(lax.rem(at, per) * tile, tile), tile)
    query = own_ref[at // per, :size, columns]
    scores = jnp.dot(rows_ref[...], query, preferred_element_type=jnp.float32)
    keys, queries = scores.shape
    live = jnp.broadcast_to(live_ref[...][:, None, :] > 0, (keys // BLOCK, BLOCK, queries))
    scores = scores.reshape(keys // BLOCK, BLOCK, queries)
    scores = jnp.where(live, scores, NEG)
    highest = jnp.max(scores, axis=(0, 1), keepdims=True)
    weights = jnp.where(live, jnp.exp((scores - highest) * scale), 0.0)
    totals = jnp.sum(weights, axis=(0, 1), keepdims=True)[0]
    weights = weights.reshape(keys, queries).astype(jnp.bfloat16)
    mixed = jnp.dot(value_ref[...], weights, preferred_element_type=jnp.float32)
    out_ref[0] = (mixed / totals).astype(jnp.bfloat16)


def attention(own, other, live):
    _, triple, step = own.shape
    size, tile = triple // 3, 128
    per = step // tile
    return pl.pallas_call(
        lambda *refs: attention_kernel(1.0 / math.sqrt(size), *refs),
        grid=(2 * per,),
        in_specs=[
            pl.BlockSpec(own.shape, lambda i: (0, 0, 0)),
            pl.BlockSpec(other.shape, lambda i: (0, 0, 0)),
            pl.BlockSpec((live.shape[0], tile), lambda i: (0, i)),
        ],
        out_specs=pl.BlockSpec((1, size, tile), lambda i: (i // per, 0, i % per)),
        out_shape=jax.ShapeDtypeStruct((2, size, step), jnp.bfloat16),
        scratch_shapes=[
            pltpu.VMEM((4 * step, size), jnp.bfloat16),
            pltpu.VMEM((size, 4 * step), jnp.bfloat16),
        ],
        name="attention",
    )(own, other, live)


def at_index(array, index, axis=0):
    return lax.dynamic_index_in_dim(array, index, axis=axis, keepdims=False)


def other_core(y, x, core):
    return y, x, 1 - core


def pair(y, x, core):
    return y ^ 1, x, core


def by_two(y, x, core):
    return y ^ 2, x, core


def around(y, x, core):
    return y, (x + 1 - 2 * core) % 4, core


def shards(section_input, norm_gain, qkv_weight, out_weight, random_blocks, global_blocks):
    yl, x, core, seq = (lax.axis_index(axis) for axis in PLANE)
    f32, bf16 = jnp.float32, jnp.bfloat16
    tokens_t = section_input[0].T
    part, length = tokens_t.shape
    step = length // 2
    width = part * 32
    first = yl // 2

    halves = tokens_t[:, :step], tokens_t[:, step:]
    own = jnp.where(core == 0, halves[0], halves[1])
    beside = moved(jnp.where(core == 0, halves[1], halves[0]), other_core)
    item = jnp.concatenate([own, beside], axis=0)

    e = moved(item, swap_inner)
    f = moved(e, by_two)
    e = jnp.concatenate([e, moved(e, pair)], axis=0)
    f = jnp.concatenate([f, moved(f, pair)], axis=0)

    as_float = item.astype(f32)
    squares = jnp.sum(as_float * as_float, axis=0).reshape(2, step // 2)
    gain = jnp.concatenate([norm_gain, moved(norm_gain, other_core)], axis=1).astype(f32)
    slot = (yl * 4 + x == jnp.arange(16))[:, None]
    lanes = 384
    table = jnp.concatenate(
        [
            jnp.pad(jnp.where(slot, gain, 0.0), ((0, 0), (0, lanes - 2 * part))),
            jnp.pad(squares, ((0, 0), (0, lanes - step // 2))),
        ],
        axis=0,
    )
    for where in (
        lambda y, x, c: (y, x ^ 1, c),
        lambda y, x, c: (y, x ^ 2, c),
        pair,
        by_two,
    ):
        table = table + moved(table, where)
    mine = table[16:, : step // 2]
    theirs = moved(mine, other_seq)
    factors = []
    for which in (mine, theirs):
        factors.append(lax.rsqrt(which.reshape(1, step) / width + 1e-05))
    factor_e = jnp.where(first == seq, factors[0], factors[1])
    factor_f = jnp.where(first == seq, factors[1], factors[0])
    gains = table[:16, : 2 * part].reshape(2, 2, 4, 2 * part)
    gains = at_index(gains, seq)

    weight = qkv_weight[0]
    beside = moved(weight, other_core)
    columns = weight.shape[1]
    weight = jnp.concatenate(
        [jnp.where(core == seq, weight, beside), jnp.where(core == seq, beside, weight)], axis=1
    )
    weight = weight.reshape(2, 4, 2, part, 2 * columns)
    weights, scales = [], []
    for k in range(4):
        source = (x - (1 - 2 * core) * k) % 4
        rows, scale = [], []
        for ab in range(2):
            which = ab ^ (yl % 2)
            block = at_index(at_index(weight, which), source)
            rows += [at_index(block, core), at_index(block, 1 - core)]
            scale.append(at_index(at_index(gains, which), source))
        weights.append(jnp.concatenate(rows, axis=0).T)
        scales.append(jnp.concatenate(scale).reshape(4 * part, 1))

    def project(block, k, factor):
        normed = (block.astype(f32) * factor * scales[k]).astype(bf16)
        return jnp.dot(weights[k], normed, preferred_element_type=f32)

    out_t = out_weight[0].T.reshape(part, 4, 4, -1)
    per = out_t.shape[3]
    out_cols = []
    for r in range(4):
        block = at_index(out_t, (x + r) % 4, axis=2).reshape(part, 4 * per)
        if r:
            block = moved(block, lambda y, x, c, r=r: (y, (x + r) % 4, c))
        out_cols.append(block)
    out_cols = jnp.stack(out_cols)
    out_cols = jnp.stack([out_cols, moved(out_cols, other_core)], axis=1)
    out_cols = out_cols.reshape(8 * part, 4, per)

    rows = jnp.stack([random_blocks[0], moved(random_blocks[0], other_seq)])
    rows = jnp.where(first == seq, rows, rows[::-1])
    count = step // BLOCK
    rows = lax.dynamic_slice_in_dim(rows, core * count, count, axis=1).reshape(2 * count, -1)
    halves = jnp.stack([first, 1 - first]) * 2 * count
    spot = jnp.arange(count, dtype=jnp.int32)
    query_ids = (halves[:, None] + core * count + spot[None, :]).reshape(-1)
    other_ids = (halves[:, None] + (1 - core) * count + spot[None, :]).reshape(-1)
    key_ids = jnp.concatenate([query_ids, other_ids])
    allowed = block_mask(query_ids, rows, global_blocks[0], key_ids)
    live = jnp.repeat(allowed.T.astype(f32), BLOCK, axis=1)

    partial_e, partial_f = project(e, 0, factor_e), project(f, 0, factor_f)
    for k in range(1, 4):
        e, f = moved(e, around), moved(f, around)
        partial_e = partial_e + project(e, k, factor_e)
        partial_f = partial_f + project(f, k, factor_f)
    joined = []
    for partial in (partial_e, partial_f):
        came = moved(partial[columns:].astype(bf16), other_seq)
        joined.append((partial[:columns] + came.astype(f32)).astype(bf16))
    joined = jnp.stack(joined)
    head = columns // 3
    attended = attention(joined, moved(joined[:, head:], other_core), live)

    kept = jnp.where(first == seq, attended[0], attended[1])
    came = moved(jnp.where(first == seq, attended[1], attended[0]), other_seq)
    heads = jnp.where(
        seq == 0,
        jnp.concatenate([kept, came], axis=0),
        jnp.concatenate([came, kept], axis=0),
    )
    far = moved(heads, by_two)
    blocks = [(heads, yl), (far, yl ^ 2), (moved(heads, pair), yl ^ 1), (moved(far, pair), yl ^ 3)]
    added = 0.0
    for block, row in blocks:
        added = added + jnp.dot(at_index(out_cols, row, axis=1), block, preferred_element_type=f32)
    added = added.reshape(4, 2 * part, step)
    total = added[0]
    for r in range(1, 4):
        total = total + moved(
            added[r].astype(bf16), lambda y, x, c, r=r: (y, (x - r) % 4, c)
        ).astype(f32)
    result = (as_float + total).astype(bf16)

    sections = lax.axis_size("section")
    straight = [(i * 2 + c, (i + 1) % sections * 2 + c) for i in range(sections) for c in range(2)]
    across = [(a, b ^ 1) for a, b in straight]
    straight = lax.ppermute(result[:part], ("section", "core"), straight)
    across = lax.ppermute(result[part:], ("section", "core"), across)
    handed_on = jnp.where(
        core == 0,
        jnp.concatenate([straight, across], axis=1),
        jnp.concatenate([across, straight], axis=1),
    )
    return handed_on.T[None]


def solution(mesh):
    fine = Mesh(mesh.devices.reshape(8, 4, 4, 2, 2), ("section", "yl", "x", "core", "seq"))
    placed = (
        P("section", "seq", DP),
        P("section", DP),
        P("section", "seq", DP),
        P("section", None, DP),
        P("section", "seq", None),
        P("section", None),
    )
    return jax.shard_map(
        shards, mesh=fine, in_specs=placed, out_specs=P("section", "seq", DP), check_vma=False
    )
```

```python
import math

import jax
import jax.numpy as jnp
from jax import lax
from jax.experimental import pallas as pl
from jax.experimental.pallas import tpu as pltpu
from jax.sharding import Mesh, PartitionSpec as P

BLOCK = 64
PLANE = ("yl", "x", "core", "seq")
DP = ("yl", "x", "core")
NEG = -1e30


def pairs_of(where):
    pairs = []
    for yl in range(4):
        for x in range(4):
            for core in range(2):
                for seq in range(2):
                    target = where(seq * 4 + yl, x, core)
                    if target is None:
                        continue
                    ty, tx, tc = target
                    source_at = ((yl * 4 + x) * 2 + core) * 2 + seq
                    target_at = (((ty % 4) * 4 + tx) * 2 + tc) * 2 + ty // 4
                    pairs.append((source_at, target_at))
    return pairs


def moved(value, where):
    return lax.ppermute(value, PLANE, pairs_of(where))


def moved_on(value, where):
    sections, plane = lax.axis_size("section"), 64
    pairs = [
        (i * plane + a, (i + 1) % sections * plane + b)
        for i in range(sections)
        for a, b in pairs_of(where)
    ]
    return lax.ppermute(value, ("section", *PLANE), pairs)


def swap_inner(y, x, core):
    if y in (2, 3):
        return y + 2, x, core
    if y in (4, 5):
        return y - 2, x, core
    return y, x, core


def other_seq(y, x, core):
    return (y + 4) % 8, x, core


def block_mask(query_ids, random_rows, global_ids, key_ids):
    query_col = query_ids[:, None]
    key_ids = key_ids[None, :]
    adjacent = jnp.abs(query_col - key_ids) <= 1
    key_global = jnp.any(key_ids[:, :, None] == global_ids[None, None, :], axis=2)
    query_global = jnp.any(query_col[:, :, None] == global_ids[None, None, :], axis=2)
    chosen = jnp.any(random_rows[:, None, :] == key_ids[:, :, None], axis=2)
    return adjacent | key_global | query_global | chosen


def attention_kernel(scale, query_ref, own_ref, other_ref, live_ref, out_ref, rows_ref, value_ref):
    size = query_ref.shape[0]

    @pl.when(pl.program_id(0) == 0)
    def _():
        step = own_ref.shape[2]
        for i in range(2):
            here, there = pl.ds(i * step, step), pl.ds((2 + i) * step, step)
            rows_ref[here, :] = own_ref[i, size : 2 * size, :].T
            rows_ref[there, :] = other_ref[i, :size, :].T
            value_ref[:, here] = own_ref[i, 2 * size :, :]
            value_ref[:, there] = other_ref[i, size:, :]

    scores = jnp.dot(rows_ref[...], query_ref[...], preferred_element_type=jnp.float32)
    keys, queries = scores.shape
    live = jnp.broadcast_to(live_ref[...][:, None, :] > 0, (keys // BLOCK, BLOCK, queries))
    scores = scores.reshape(keys // BLOCK, BLOCK, queries)
    scores = jnp.where(live, scores, NEG)
    highest = jnp.max(scores, axis=(0, 1), keepdims=True)
    weights = jnp.where(live, jnp.exp((scores - highest) * scale), 0.0)
    totals = jnp.sum(weights, axis=(0, 1), keepdims=True)[0]
    weights = weights.reshape(keys, queries).astype(jnp.bfloat16)
    mixed = jnp.dot(value_ref[...], weights, preferred_element_type=jnp.float32)
    out_ref[...] = (mixed / totals).astype(jnp.bfloat16)


def attention(query, own, other, live, at):
    size, step = query.shape
    tile = 128
    per = step // tile
    return pl.pallas_call(
        lambda *refs: attention_kernel(1.0 / math.sqrt(size), *refs),
        grid=(per,),
        in_specs=[
            pl.BlockSpec((size, tile), lambda i: (0, i)),
            pl.BlockSpec(own.shape, lambda i: (0, 0, 0)),
            pl.BlockSpec(other.shape, lambda i: (0, 0, 0)),
            pl.BlockSpec((live.shape[0], tile), lambda i: (0, at * per + i)),
        ],
        out_specs=pl.BlockSpec((size, tile), lambda i: (0, i)),
        out_shape=jax.ShapeDtypeStruct(query.shape, jnp.bfloat16),
        scratch_shapes=[
            pltpu.VMEM((4 * step, size), jnp.bfloat16),
            pltpu.VMEM((size, 4 * step), jnp.bfloat16),
        ],
        cost_estimate=pl.CostEstimate(
            flops=16 * size * step * step, bytes_accessed=6 * size * step, transcendentals=4 * step * step
        ),
        name="attention",
    )(query, own, other, live)


def slices_kernel(at_ref, source_ref, out_ref, sems):
    rings, _, width = out_ref.shape
    per = width // 4
    copies = []
    for r in range(rings):
        for p in range(4):
            start = pl.multiple_of(at_ref[r * 4 + p] * per, per)
            copies.append(
                pltpu.make_async_copy(
                    source_ref.at[:, pl.ds(start, per)],
                    out_ref.at[r, :, pl.ds(p * per, per)],
                    sems.at[r * 4 + p],
                )
            )
    for copy in copies:
        copy.start()
    for copy in copies:
        copy.wait()


def column_slices(matrix, at):
    rows, width = matrix.shape
    return pl.pallas_call(
        slices_kernel,
        in_specs=[pl.BlockSpec(memory_space=pltpu.SMEM), pl.BlockSpec(memory_space=pl.ANY)],
        out_specs=pl.BlockSpec(memory_space=pl.ANY),
        out_shape=jax.ShapeDtypeStruct((4, rows, width // 4), matrix.dtype),
        scratch_shapes=[pltpu.SemaphoreType.DMA((16,))],
        cost_estimate=pl.CostEstimate(
            flops=0, bytes_accessed=4 * rows * width, transcendentals=0
        ),
        name="column_slices",
    )(at, matrix)


def at_index(array, index, axis=0):
    return lax.dynamic_index_in_dim(array, index, axis=axis, keepdims=False)


def other_core(y, x, core):
    return y, x, 1 - core


def pair(y, x, core):
    return y ^ 1, x, core


def by_two(y, x, core):
    return y ^ 2, x, core


def around(y, x, core):
    return y, (x + 1 - 2 * core) % 4, core


def same(y, x, core):
    return y, x, core


def shards(section_input, norm_gain, qkv_weight, out_weight, random_blocks, global_blocks):
    yl, x, core, seq = (lax.axis_index(axis) for axis in PLANE)
    f32, bf16 = jnp.float32, jnp.bfloat16
    tokens_t = section_input[0].T
    part, length = tokens_t.shape
    step = length // 2
    width = part * 32
    first = yl // 2

    def of_core(array):
        halves = array[:, :step], array[:, step:]
        return jnp.where(core == 0, *halves), jnp.where(core == 0, *halves[::-1])

    top = float(jnp.finfo(bf16).max)
    gained = tokens_t.astype(f32) * norm_gain.astype(f32).T
    gained = jnp.clip(gained, -top, top).astype(bf16)
    own, away = of_core(gained)
    crossed = moved(away, lambda *at: other_core(*swap_inner(*at)))
    e = jnp.concatenate([moved(own, swap_inner), crossed], axis=0)
    f = moved(e, by_two)
    e_pair = moved(e, pair)
    e = jnp.concatenate([e, e_pair], axis=0)
    f = jnp.concatenate([f, moved(f, pair)], axis=0)

    own, away = of_core(tokens_t)
    item = jnp.concatenate([own, moved(away, other_core)], axis=0)
    as_float = item.astype(f32)
    squares = jnp.sum(as_float * as_float, axis=0).reshape(step // 128, 128)
    squares = jnp.concatenate([squares, moved(squares, other_seq)], axis=0)
    for where in (
        lambda y, x, c: (y, x ^ 1, c),
        lambda y, x, c: (y, x ^ 2, c),
        pair,
        by_two,
    ):
        squares = squares + moved(squares, where)
    factors = lax.rsqrt(squares.reshape(2, 1, step) / width + 1e-05)
    factor_e = jnp.where(first == seq, factors[0], factors[1])
    factor_f = jnp.where(first == seq, factors[1], factors[0])

    out_t = out_weight[0].T
    order = jnp.stack([yl, yl ^ 2, yl ^ 1, yl ^ 3])
    ring = (x + jnp.arange(4, dtype=jnp.int32)) % 4
    slices = column_slices(out_t, (order[None, :] * 4 + ring[:, None]).reshape(-1))
    out_cols = jnp.stack(
        [moved_on(slices[r], lambda y, x, c, r=r: (y, (x + r) % 4, c)) for r in range(4)]
    )
    out_cols = jnp.stack([out_cols, moved(out_cols, other_core)])
    out_cols = out_cols.reshape(8 * part, -1)
    residual = moved_on(item, same)

    weight = qkv_weight[0]
    beside = moved(weight, other_core)
    columns = weight.shape[1]
    weight = jnp.concatenate(
        [jnp.where(core == seq, weight, beside), jnp.where(core == seq, beside, weight)], axis=1
    )
    weight = weight.reshape(2, 4, 2, part, 2 * columns)
    weights = []
    for k in range(4):
        source = (x - (1 - 2 * core) * k) % 4
        rows = []
        for ab in range(2):
            block = at_index(at_index(weight, ab ^ (yl % 2)), source)
            rows += [at_index(block, core), at_index(block, 1 - core)]
        weights.append(jnp.concatenate(rows, axis=0).T)

    def project(block, k, factor):
        normed = (block.astype(f32) * factor).astype(bf16)
        return jnp.dot(weights[k], normed, preferred_element_type=f32)

    count = step // BLOCK
    rows = jnp.stack([moved(random_blocks[0], other_seq), random_blocks[0]])
    rows = lax.dynamic_slice_in_dim(rows, core * count, count, axis=1).reshape(2 * count, -1)
    spot = jnp.arange(count, dtype=jnp.int32)

    def block_ids(halves, core):
        halves = jnp.stack(halves) * 2 * count
        return (halves[:, None] + core * count + spot[None, :]).reshape(-1)

    query_ids = block_ids([1 - seq, seq], core)
    key_ids = jnp.concatenate(
        [block_ids([first, 1 - first], core), block_ids([first, 1 - first], 1 - core)]
    )
    allowed = block_mask(query_ids, rows, global_blocks[0], key_ids)
    live = jnp.repeat(allowed.T.astype(f32), BLOCK, axis=1)

    partial_e, partial_f = project(e, 0, factor_e), project(f, 0, factor_f)
    for k in range(1, 4):
        e, f = moved(e, around), moved(f, around)
        partial_e = partial_e + project(e, k, factor_e)
        partial_f = partial_f + project(f, k, factor_f)
    joined = []
    for partial in (partial_e, partial_f):
        came = moved(partial[columns:].astype(bf16), other_seq)
        joined.append((partial[:columns] + came.astype(f32)).astype(bf16))
    head = columns // 3
    query_sent = jnp.where(first == seq, joined[1][:head], joined[0][:head])
    query_kept = jnp.where(first == seq, joined[0][:head], joined[1][:head])
    joined = jnp.stack(joined)
    other = moved(joined[:, head:], other_core)
    came = moved_on(attention(query_sent, joined, other, live, 0), other_seq)
    kept = moved_on(attention(query_kept, joined, other, live, 1), same)

    heads = jnp.concatenate(
        [jnp.where(seq == 0, kept, came), jnp.where(seq == 0, came, kept)], axis=0
    )
    far = moved(heads, by_two)
    blocks = [heads, far, moved(heads, pair), moved(far, pair)]
    per = heads.shape[0]
    added = 0.0
    for p, block in enumerate(blocks):
        added = added + jnp.dot(
            out_cols[:, p * per : (p + 1) * per], block, preferred_element_type=f32
        )
    added = added.reshape(2, 4, part, step)
    total = residual.astype(f32) + added[:, 0].reshape(2 * part, step)
    for r in range(1, 4):
        share = added[:, r].reshape(2 * part, step).astype(bf16)
        total = total + moved(share, lambda y, x, c, r=r: (y, (x - r) % 4, c)).astype(f32)
    result = total.astype(bf16)

    own, away = result[:part], moved(result[part:], other_core)
    handed_on = jnp.concatenate(
        [jnp.where(core == 0, own, away), jnp.where(core == 0, away, own)], axis=1
    )
    return handed_on.T[None]


def solution(mesh):
    fine = Mesh(mesh.devices.reshape(8, 4, 4, 2, 2), ("section", "yl", "x", "core", "seq"))
    placed = (
        P("section", "seq", DP),
        P("section", DP),
        P("section", "seq", DP),
        P("section", None, DP),
        P("section", "seq", None),
        P("section", None),
    )
    return jax.shard_map(
        shards, mesh=fine, in_specs=placed, out_specs=P("section", "seq", DP), check_vma=False
    )
```

```python
import math

import jax
import jax.numpy as jnp
from jax import lax
from jax.experimental import pallas as pl
from jax.experimental.pallas import tpu as pltpu
from jax.sharding import Mesh, PartitionSpec as P

BLOCK = 64
PLANE = ("yl", "x", "core", "seq")
DP = ("yl", "x", "core")
NEG = -1e30


def pairs_of(where):
    pairs = []
    for yl in range(4):
        for x in range(4):
            for core in range(2):
                for seq in range(2):
                    target = where(seq * 4 + yl, x, core)
                    if target is None:
                        continue
                    ty, tx, tc = target
                    source_at = ((yl * 4 + x) * 2 + core) * 2 + seq
                    target_at = (((ty % 4) * 4 + tx) * 2 + tc) * 2 + ty // 4
                    pairs.append((source_at, target_at))
    return pairs


def moved(value, where):
    return lax.ppermute(value, PLANE, pairs_of(where))


def moved_on(value, where):
    sections, plane = lax.axis_size("section"), 64
    pairs = [
        (i * plane + a, (i + 1) % sections * plane + b)
        for i in range(sections)
        for a, b in pairs_of(where)
    ]
    return lax.ppermute(value, ("section", *PLANE), pairs)


def swap_inner(y, x, core):
    if y in (2, 3):
        return y + 2, x, core
    if y in (4, 5):
        return y - 2, x, core
    return y, x, core


def other_seq(y, x, core):
    return (y + 4) % 8, x, core


def block_mask(query_ids, random_rows, global_ids, key_ids):
    query_col = query_ids[:, None]
    key_ids = key_ids[None, :]
    adjacent = jnp.abs(query_col - key_ids) <= 1
    key_global = jnp.any(key_ids[:, :, None] == global_ids[None, None, :], axis=2)
    query_global = jnp.any(query_col[:, :, None] == global_ids[None, None, :], axis=2)
    chosen = jnp.any(random_rows[:, None, :] == key_ids[:, :, None], axis=2)
    return adjacent | key_global | query_global | chosen


def attention_kernel(scale, query_ref, own_ref, other_ref, bias_ref, out_ref, rows_ref, value_ref, wide_ref):
    size = query_ref.shape[0]

    @pl.when(pl.program_id(0) == 0)
    def _():
        step = own_ref.shape[2]
        for i in range(2):
            here, there = pl.ds(i * step, step), pl.ds((2 + i) * step, step)
            rows_ref[here, :size] = own_ref[i, size : 2 * size, :].T
            rows_ref[there, :size] = other_ref[i, :size, :].T
            value_ref[:, here] = own_ref[i, 2 * size :, :]
            value_ref[:, there] = other_ref[i, size:, :]
        shape = (rows_ref.shape[0], size)
        block = lax.broadcasted_iota(jnp.int32, shape, 0) // BLOCK
        column = lax.broadcasted_iota(jnp.int32, shape, 1)
        rows_ref[:, size:] = jnp.where(block == column, 1.0, 0.0).astype(jnp.bfloat16)
        wide_ref[...] = jnp.zeros_like(wide_ref)

    wide_ref[:size, :] = query_ref[...]
    wide_ref[size : size + bias_ref.shape[0], :] = bias_ref[...]
    scores = jnp.dot(rows_ref[...], wide_ref[...], preferred_element_type=jnp.float32)
    highest = jnp.max(scores, axis=0, keepdims=True)
    weights = jnp.exp((scores - highest) * scale)
    totals = jnp.sum(weights, axis=0, keepdims=True)
    mixed = jnp.dot(
        value_ref[...], weights.astype(jnp.bfloat16), preferred_element_type=jnp.float32
    )
    out_ref[...] = (mixed / totals).astype(jnp.bfloat16)


def attention(query, own, other, bias, at):
    size, step = query.shape
    tile = 128
    per = step // tile
    return pl.pallas_call(
        lambda *refs: attention_kernel(1.0 / math.sqrt(size), *refs),
        grid=(per,),
        in_specs=[
            pl.BlockSpec((size, tile), lambda i: (0, i)),
            pl.BlockSpec(own.shape, lambda i: (0, 0, 0)),
            pl.BlockSpec(other.shape, lambda i: (0, 0, 0)),
            pl.BlockSpec((bias.shape[0], tile), lambda i: (0, at * per + i)),
        ],
        out_specs=pl.BlockSpec((size, tile), lambda i: (0, i)),
        out_shape=jax.ShapeDtypeStruct(query.shape, jnp.bfloat16),
        scratch_shapes=[
            pltpu.VMEM((4 * step, 2 * size), jnp.bfloat16),
            pltpu.VMEM((size, 4 * step), jnp.bfloat16),
            pltpu.VMEM((2 * size, tile), jnp.bfloat16),
        ],
        cost_estimate=pl.CostEstimate(
            flops=16 * size * step * step, bytes_accessed=6 * size * step, transcendentals=4 * step * step
        ),
        name="attention",
    )(query, own, other, bias)


def slices_kernel(order_ref, ring_ref, source_ref, *out_refs):
    for r, out_ref in enumerate(out_refs):
        per = out_ref.shape[1]
        start = pl.multiple_of(ring_ref[r] * per, per)
        out_ref[...] = source_ref[:, pl.ds(start, per)]


def column_slices(matrix, order, ring):
    rows, width = matrix.shape
    block = pl.BlockSpec((rows, width // 16), lambda p, order, ring: (0, p))
    return pl.pallas_call(
        slices_kernel,
        grid_spec=pltpu.PrefetchScalarGridSpec(
            num_scalar_prefetch=2,
            grid=(4,),
            in_specs=[pl.BlockSpec((rows, width // 4), lambda p, order, ring: (0, order[p]))],
            out_specs=[block] * 4,
        ),
        out_shape=[jax.ShapeDtypeStruct((rows, width // 4), matrix.dtype)] * 4,
        cost_estimate=pl.CostEstimate(
            flops=0, bytes_accessed=4 * rows * width, transcendentals=0
        ),
        name="column_slices",
    )(order, ring, matrix)


def rows_kernel(*refs):
    *parts, out_ref = refs
    start = 0
    for part in parts:
        out_ref[start : start + part.shape[0], :] = part[...]
        start += part.shape[0]


def stacked_rows(*parts):
    rows = sum(part.shape[0] for part in parts)
    vmem = pl.BlockSpec(memory_space=pltpu.VMEM)
    return pl.pallas_call(
        rows_kernel,
        in_specs=[vmem] * len(parts),
        out_specs=vmem,
        out_shape=jax.ShapeDtypeStruct((rows, parts[0].shape[1]), parts[0].dtype),
        cost_estimate=pl.CostEstimate(
            flops=0, bytes_accessed=4 * rows * parts[0].shape[1], transcendentals=0
        ),
        name="stacked_rows",
    )(*parts)


def after(value, earlier):
    return lax.optimization_barrier((value, earlier))[0]


def at_index(array, index, axis=0):
    return lax.dynamic_index_in_dim(array, index, axis=axis, keepdims=False)


def other_core(y, x, core):
    return y, x, 1 - core


def pair(y, x, core):
    return y ^ 1, x, core


def by_two(y, x, core):
    return y ^ 2, x, core


def around(y, x, core):
    return y, (x + 1 - 2 * core) % 4, core


def same(y, x, core):
    return y, x, core


def shards(section_input, norm_gain, qkv_weight, out_weight, random_blocks, global_blocks):
    yl, x, core, seq = (lax.axis_index(axis) for axis in PLANE)
    f32, bf16 = jnp.float32, jnp.bfloat16
    tokens_t = section_input[0].T
    part, length = tokens_t.shape
    step = length // 2
    width = part * 32
    first = yl // 2

    def of_core(array):
        halves = array[:, :step], array[:, step:]
        return jnp.where(core == 0, *halves), jnp.where(core == 0, *halves[::-1])

    own, away = of_core(tokens_t)
    crossed = moved(away, lambda *at: other_core(*swap_inner(*at)))
    e = stacked_rows(moved(own, swap_inner), crossed)
    f = moved(e, by_two)
    e_two = stacked_rows(e, moved(e, pair))
    f_two = stacked_rows(f, moved(f, pair))

    gain = norm_gain
    gain_row = jnp.pad(gain, ((0, 15), (0, step - part)))
    beside = moved(jnp.concatenate([away, gain_row], axis=0), other_core)
    gain = jnp.concatenate([gain, beside[part : part + 1, :part]], axis=1).astype(f32)
    item = jnp.concatenate([own, beside[:part]], axis=0)
    as_float = item.astype(f32)
    squares = jnp.sum(as_float * as_float, axis=0)
    random = random_blocks[0]
    numbers = jnp.pad(random.astype(f32).reshape(-1), (0, step - random.size))
    mine = jnp.stack([squares, numbers])
    theirs = moved(mine, other_seq)
    random = jnp.stack([theirs[1, : random.size].astype(jnp.int32).reshape(random.shape), random])
    slot = (yl * 4 + x == jnp.arange(16))[:, None]
    table = jnp.where(slot, jnp.pad(gain, ((0, 0), (0, step - 2 * part))), 0.0)
    table = jnp.concatenate([table, mine[:1], theirs[:1]], axis=0)
    for where in (
        lambda y, x, c: (y, x ^ 1, c),
        lambda y, x, c: (y, x ^ 2, c),
        pair,
        by_two,
    ):
        table = table + moved(table, where)
    factors = lax.rsqrt(table[16:] / width + 1e-05)
    factor_e = jnp.where(first == seq, factors[:1], factors[1:])
    factor_f = jnp.where(first == seq, factors[1:], factors[:1])
    gains = table[:16, : 2 * part].reshape(2, 2, 4, 2 * part)
    gains = at_index(gains, seq)

    weight = after(qkv_weight[0], beside)
    beside = moved(weight, other_core)
    columns = weight.shape[1]
    weight = jnp.concatenate(
        [jnp.where(core == seq, weight, beside), jnp.where(core == seq, beside, weight)], axis=1
    )
    weight = weight.reshape(2, 4, 2, part, 2 * columns)
    weights, scales = [], []
    for k in range(4):
        source = (x - (1 - 2 * core) * k) % 4
        rows, scale = [], []
        for ab in range(2):
            which = ab ^ (yl % 2)
            block = at_index(at_index(weight, which), source)
            rows += [at_index(block, core), at_index(block, 1 - core)]
            scale.append(at_index(at_index(gains, which), source))
        weights.append(jnp.concatenate(rows, axis=0).T)
        scales.append(jnp.concatenate(scale).reshape(4 * part, 1))

    order = after(jnp.stack([yl, yl ^ 2, yl ^ 1, yl ^ 3]), e)
    ring = (x + jnp.arange(4, dtype=jnp.int32)) % 4
    slices = column_slices(out_weight[0].T, order, ring)
    laid = jnp.concatenate([item[:part], item[part:]], axis=1)
    ahead = moved_on(stacked_rows(slices[0], laid), same)
    residual = ahead[part:]
    out_own = [ahead[:part]]
    for r in range(1, 4):
        out_own.append(moved_on(slices[r], lambda y, x, c, r=r: (y, (x + r) % 4, c)))
    out_own = stacked_rows(*out_own)
    out_cols = out_own, moved(out_own, other_core)

    def project(block, k, factor):
        normed = (block.astype(f32) * factor * scales[k]).astype(bf16)
        return jnp.dot(weights[k], normed, preferred_element_type=f32)

    count = step // BLOCK
    rows = lax.dynamic_slice_in_dim(random, core * count, count, axis=1).reshape(2 * count, -1)
    spot = jnp.arange(count, dtype=jnp.int32)

    def block_ids(halves, core):
        halves = jnp.stack(halves) * 2 * count
        return (halves[:, None] + core * count + spot[None, :]).reshape(-1)

    query_ids = block_ids([1 - seq, seq], core)
    key_ids = jnp.concatenate(
        [block_ids([first, 1 - first], core), block_ids([first, 1 - first], 1 - core)]
    )
    allowed = block_mask(query_ids, rows, global_blocks[0], key_ids)
    bias = jnp.repeat(jnp.where(allowed.T, 0.0, NEG), BLOCK, axis=1).astype(bf16)

    e, f = e_two, f_two
    partial_e, partial_f = project(e, 0, factor_e), project(f, 0, factor_f)
    for k in range(1, 4):
        e, f = moved(e, around), moved(f, around)
        partial_e = partial_e + project(e, k, factor_e)
        partial_f = partial_f + project(f, k, factor_f)
    joined = []
    for partial in (partial_e, partial_f):
        came = moved(partial[columns:].astype(bf16), other_seq)
        joined.append((partial[:columns] + came.astype(f32)).astype(bf16))
    head = columns // 3
    query_sent = jnp.where(first == seq, joined[1][:head], joined[0][:head])
    query_kept = jnp.where(first == seq, joined[0][:head], joined[1][:head])
    joined = jnp.stack(joined)
    other = moved(joined[:, head:], other_core)
    came = moved_on(attention(query_sent, joined, other, bias, 0), other_seq)
    kept = moved_on(attention(query_kept, joined, other, bias, 1), same)

    heads = jnp.concatenate(
        [jnp.where(seq == 0, kept, came), jnp.where(seq == 0, came, kept)], axis=0
    )
    far = moved(heads, by_two)
    blocks = [heads, far, moved(heads, pair), moved(far, pair)]
    per = heads.shape[0]
    added = []
    for cols in out_cols:
        total = 0.0
        for p, block in enumerate(blocks):
            total = total + jnp.dot(
                cols[:, p * per : (p + 1) * per], block, preferred_element_type=f32
            )
        added.append(total)
    total = jnp.concatenate([residual[:, :step], residual[:, step:]], axis=0).astype(f32)
    total = total + jnp.concatenate([half[:part] for half in added], axis=0)
    for r in range(1, 4):
        share = jnp.concatenate(
            [half[r * part : (r + 1) * part].astype(bf16) for half in added], axis=0
        )
        total = total + moved(share, lambda y, x, c, r=r: (y, (x - r) % 4, c)).astype(f32)
    result = total.astype(bf16)

    own, away = result[:part], moved(result[part:], other_core)
    handed_on = jnp.concatenate(
        [jnp.where(core == 0, own, away), jnp.where(core == 0, away, own)], axis=1
    )
    return handed_on.T[None]


def solution(mesh):
    fine = Mesh(mesh.devices.reshape(8, 4, 4, 2, 2), ("section", "yl", "x", "core", "seq"))
    placed = (
        P("section", "seq", DP),
        P("section", DP),
        P("section", "seq", DP),
        P("section", None, DP),
        P("section", "seq", None),
        P("section", None),
    )
    return jax.shard_map(
        shards, mesh=fine, in_specs=placed, out_specs=P("section", "seq", DP), check_vma=False
    )
```

```python
import math

import jax
import jax.numpy as jnp
from jax import lax
from jax.experimental import pallas as pl
from jax.experimental.pallas import tpu as pltpu
from jax.sharding import Mesh, PartitionSpec as P

BLOCK = 64
PLANE = ("yl", "x", "core", "seq")
DP = ("yl", "x", "core")
NEG = -1e30


def pairs_of(where):
    pairs = []
    for yl in range(4):
        for x in range(4):
            for core in range(2):
                for seq in range(2):
                    target = where(seq * 4 + yl, x, core)
                    if target is None:
                        continue
                    ty, tx, tc = target
                    source_at = ((yl * 4 + x) * 2 + core) * 2 + seq
                    target_at = (((ty % 4) * 4 + tx) * 2 + tc) * 2 + ty // 4
                    pairs.append((source_at, target_at))
    return pairs


def moved(value, where):
    return lax.ppermute(value, PLANE, pairs_of(where))


def moved_on(value, where):
    sections, plane = lax.axis_size("section"), 64
    pairs = [
        (i * plane + a, (i + 1) % sections * plane + b)
        for i in range(sections)
        for a, b in pairs_of(where)
    ]
    return lax.ppermute(value, ("section", *PLANE), pairs)


def swap_inner(y, x, core):
    if y in (2, 3):
        return y + 2, x, core
    if y in (4, 5):
        return y - 2, x, core
    return y, x, core


def other_seq(y, x, core):
    return (y + 4) % 8, x, core


def block_mask(query_ids, random_rows, global_ids, key_ids):
    query_col = query_ids[:, None]
    key_ids = key_ids[None, :]
    adjacent = jnp.abs(query_col - key_ids) <= 1
    key_global = jnp.any(key_ids[:, :, None] == global_ids[None, None, :], axis=2)
    query_global = jnp.any(query_col[:, :, None] == global_ids[None, None, :], axis=2)
    chosen = jnp.any(random_rows[:, None, :] == key_ids[:, :, None], axis=2)
    return adjacent | key_global | query_global | chosen


def attention_kernel(scale, per, flag_ref, *refs):
    own_refs, other_refs = refs[:2], refs[2:4]
    bias_ref, sent_ref, kept_ref, rows_ref, value_ref, wide_ref = refs[4:]
    size, tile = sent_ref.shape
    at = pl.program_id(0)

    @pl.when(at == 0)
    def _():
        step = per * tile
        for i in range(2):
            here, there = pl.ds(i * step, step), pl.ds((2 + i) * step, step)
            rows_ref[here, :size] = own_refs[i][size : 2 * size, :].T
            rows_ref[there, :size] = other_refs[i][:size, :].T
            value_ref[:, here] = own_refs[i][2 * size :, :]
            value_ref[:, there] = other_refs[i][size:, :]
        shape = (rows_ref.shape[0], size)
        block = lax.broadcasted_iota(jnp.int32, shape, 0) // BLOCK
        column = lax.broadcasted_iota(jnp.int32, shape, 1)
        rows_ref[:, size:] = jnp.where(block == column, 1.0, 0.0).astype(jnp.bfloat16)
        wide_ref[...] = jnp.zeros_like(wide_ref)

    columns = pl.ds(pl.multiple_of(lax.rem(at, per) * tile, tile), tile)
    use_f = (at < per) == (flag_ref[0] > 0)

    @pl.when(use_f)
    def _():
        wide_ref[:size, :] = own_refs[1][:size, columns]

    @pl.when(jnp.logical_not(use_f))
    def _():
        wide_ref[:size, :] = own_refs[0][:size, columns]

    wide_ref[size : size + bias_ref.shape[0], :] = bias_ref[...]
    scores = jnp.dot(rows_ref[...], wide_ref[...], preferred_element_type=jnp.float32)
    highest = jnp.max(scores, axis=0, keepdims=True)
    weights = jnp.exp((scores - highest) * scale)
    totals = jnp.sum(weights, axis=0, keepdims=True)
    mixed = jnp.dot(
        value_ref[...], weights.astype(jnp.bfloat16), preferred_element_type=jnp.float32
    )
    mixed = (mixed / totals).astype(jnp.bfloat16)

    @pl.when(at < per)
    def _():
        sent_ref[...] = mixed

    @pl.when(at >= per)
    def _():
        kept_ref[...] = mixed


def attention(flag, own, other, bias):
    triple, step = own[0].shape
    size, tile = triple // 3, 256
    per = step // tile

    def whole(array):
        return pl.BlockSpec(array.shape, lambda i, flag: (0, 0))

    return pl.pallas_call(
        lambda *refs: attention_kernel(1.0 / math.sqrt(size), per, *refs),
        grid_spec=pltpu.PrefetchScalarGridSpec(
            num_scalar_prefetch=1,
            grid=(2 * per,),
            in_specs=[whole(array) for array in (*own, *other)]
            + [pl.BlockSpec((bias.shape[0], tile), lambda i, flag: (0, i))],
            out_specs=[
                pl.BlockSpec((size, tile), lambda i, flag: (0, jnp.minimum(i, per - 1))),
                pl.BlockSpec((size, tile), lambda i, flag: (0, jnp.maximum(i - per, 0))),
            ],
            scratch_shapes=[
                pltpu.VMEM((4 * step, 2 * size), jnp.bfloat16),
                pltpu.VMEM((size, 4 * step), jnp.bfloat16),
                pltpu.VMEM((2 * size, tile), jnp.bfloat16),
            ],
        ),
        out_shape=[jax.ShapeDtypeStruct((size, step), jnp.bfloat16)] * 2,
        cost_estimate=pl.CostEstimate(
            flops=32 * size * step * step, bytes_accessed=12 * size * step, transcendentals=8 * step * step
        ),
        name="attention",
    )(flag, *own, *other, bias)


def slices_kernel(order_ref, ring_ref, source_ref, *out_refs):
    for r, out_ref in enumerate(out_refs):
        per = out_ref.shape[1]
        start = pl.multiple_of(ring_ref[r] * per, per)
        out_ref[...] = source_ref[:, pl.ds(start, per)]


def column_slices(matrix, order, ring):
    rows, width = matrix.shape
    block = pl.BlockSpec((rows, width // 16), lambda p, order, ring: (0, p))
    return pl.pallas_call(
        slices_kernel,
        grid_spec=pltpu.PrefetchScalarGridSpec(
            num_scalar_prefetch=2,
            grid=(4,),
            in_specs=[pl.BlockSpec((rows, width // 4), lambda p, order, ring: (0, order[p]))],
            out_specs=[block] * 4,
        ),
        out_shape=[jax.ShapeDtypeStruct((rows, width // 4), matrix.dtype)] * 4,
        cost_estimate=pl.CostEstimate(
            flops=0, bytes_accessed=4 * rows * width, transcendentals=0
        ),
        name="column_slices",
    )(order, ring, matrix)


def rows_kernel(*refs):
    *parts, out_ref = refs
    start = 0
    for part in parts:
        out_ref[start : start + part.shape[0], :] = part[...]
        start += part.shape[0]


def stacked_rows(*parts):
    rows = sum(part.shape[0] for part in parts)
    vmem = pl.BlockSpec(memory_space=pltpu.VMEM)
    return pl.pallas_call(
        rows_kernel,
        in_specs=[vmem] * len(parts),
        out_specs=vmem,
        out_shape=jax.ShapeDtypeStruct((rows, parts[0].shape[1]), parts[0].dtype),
        cost_estimate=pl.CostEstimate(
            flops=0, bytes_accessed=4 * rows * parts[0].shape[1], transcendentals=0
        ),
        name="stacked_rows",
    )(*parts)


def after(value, earlier):
    return lax.optimization_barrier((value, earlier))[0]


def at_index(array, index, axis=0):
    return lax.dynamic_index_in_dim(array, index, axis=axis, keepdims=False)


def other_core(y, x, core):
    return y, x, 1 - core


def pair(y, x, core):
    return y ^ 1, x, core


def by_two(y, x, core):
    return y ^ 2, x, core


def around(y, x, core):
    return y, (x + 1 - 2 * core) % 4, core


def same(y, x, core):
    return y, x, core


def shards(section_input, norm_gain, qkv_weight, out_weight, random_blocks, global_blocks):
    yl, x, core, seq = (lax.axis_index(axis) for axis in PLANE)
    f32, bf16 = jnp.float32, jnp.bfloat16
    tokens_t = section_input[0].T
    part, length = tokens_t.shape
    step = length // 2
    width = part * 32
    first = yl // 2

    def of_core(array):
        halves = array[:, :step], array[:, step:]
        return jnp.where(core == 0, *halves), jnp.where(core == 0, *halves[::-1])

    own, away = of_core(tokens_t)
    crossed = moved(away, lambda *at: other_core(*swap_inner(*at)))
    e = stacked_rows(moved(own, swap_inner), crossed)
    out_next = moved_on(out_weight[0].T, same)

    gain = norm_gain
    gain_row = jnp.pad(gain, ((0, 15), (0, step - part)))
    beside = moved(jnp.concatenate([away, gain_row], axis=0), other_core)
    gain = jnp.concatenate([gain, beside[part : part + 1, :part]], axis=1).astype(f32)
    item = jnp.concatenate([own, beside[:part]], axis=0)
    as_float = item.astype(f32)
    squares = jnp.sum(as_float * as_float, axis=0)
    residual = moved_on(item, same)
    random = random_blocks[0]
    numbers = jnp.pad(random.astype(f32).reshape(-1), (0, step - random.size))
    mine = jnp.stack([squares, numbers])
    theirs = moved(mine, other_seq)
    random = jnp.stack([theirs[1, : random.size].astype(jnp.int32).reshape(random.shape), random])
    slot = (yl * 4 + x == jnp.arange(16))[:, None]
    table = jnp.where(slot, jnp.pad(gain, ((0, 0), (0, step - 2 * part))), 0.0)
    table = jnp.concatenate([table, mine[:1], theirs[:1]], axis=0)
    table = table + moved(table, lambda y, x, c: (y, x ^ 1, c))
    e = after(e, table)
    f = moved(e, by_two)
    e_two = stacked_rows(e, moved(e, pair))
    f_two = stacked_rows(f, moved(f, pair))
    for where in (lambda y, x, c: (y, x ^ 2, c), pair, by_two):
        table = table + moved(table, where)
    factors = lax.rsqrt(table[16:] / width + 1e-05)
    factor_e = jnp.where(first == seq, factors[:1], factors[1:])
    factor_f = jnp.where(first == seq, factors[1:], factors[:1])
    gains = table[:16, : 2 * part].reshape(2, 2, 4, 2 * part)
    gains = at_index(gains, seq)

    weight = after(qkv_weight[0], beside)
    beside = moved(weight, other_core)
    columns = weight.shape[1]
    weight = jnp.concatenate(
        [jnp.where(core == seq, weight, beside), jnp.where(core == seq, beside, weight)], axis=1
    )
    weight = weight.reshape(2, 4, 2, part, 2 * columns)
    weights, scales = [], []
    for k in range(4):
        source = (x - (1 - 2 * core) * k) % 4
        rows, scale = [], []
        for ab in range(2):
            which = ab ^ (yl % 2)
            block = at_index(at_index(weight, which), source)
            rows += [at_index(block, core), at_index(block, 1 - core)]
            scale.append(at_index(at_index(gains, which), source))
        weights.append(jnp.concatenate(rows, axis=0).T)
        scales.append(jnp.concatenate(scale).reshape(4 * part, 1))

    def project(block, k, factor):
        normed = (block.astype(f32) * factor * scales[k]).astype(bf16)
        return jnp.dot(weights[k], normed, preferred_element_type=f32)

    count = step // BLOCK
    rows = lax.dynamic_slice_in_dim(random, core * count, count, axis=1).reshape(2 * count, -1)
    spot = jnp.arange(count, dtype=jnp.int32)

    def block_ids(halves, core):
        halves = jnp.stack(halves) * 2 * count
        return (halves[:, None] + core * count + spot[None, :]).reshape(-1)

    query_ids = block_ids([1 - seq, seq], core)
    key_ids = jnp.concatenate(
        [block_ids([first, 1 - first], core), block_ids([first, 1 - first], 1 - core)]
    )
    allowed = block_mask(query_ids, rows, global_blocks[0], key_ids)
    bias = jnp.repeat(jnp.where(allowed.T, 0.0, NEG), BLOCK, axis=1).astype(bf16)

    e, f = e_two, f_two
    partial_e, partial_f = project(e, 0, factor_e), project(f, 0, factor_f)
    for k in range(1, 4):
        e, f = moved(e, around), moved(f, around)
        partial_e = partial_e + project(e, k, factor_e)
        partial_f = partial_f + project(f, k, factor_f)
    order = after(jnp.stack([yl, yl ^ 2, yl ^ 1, yl ^ 3]), f_two)
    ring = (x + jnp.arange(4, dtype=jnp.int32)) % 4
    slices = column_slices(out_next, order, ring)
    sends = [partial[columns:].astype(bf16) for partial in (partial_e, partial_f)]
    sends[0], slices = lax.optimization_barrier((sends[0], slices))
    out_own = [slices[0]]
    for r in range(1, 4):
        out_own.append(moved(slices[r], lambda y, x, c, r=r: (y, (x + r) % 4, c)))
    joined, other = [], []
    head = columns // 3
    for partial, send in zip((partial_e, partial_f), sends):
        came = moved(send, other_seq)
        joined.append((partial[:columns] + came.astype(f32)).astype(bf16))
        other.append(moved(joined[-1][head:], other_core))

    flag = after((first == seq).astype(jnp.int32).reshape(1), (out_own, residual))
    out_own = stacked_rows(*out_own)
    out_cols = out_own, moved(out_own, other_core)
    sent, kept = attention(flag, joined, other, bias)
    came, kept = moved_on(sent, other_seq), moved_on(kept, same)

    heads = jnp.concatenate(
        [jnp.where(seq == 0, kept, came), jnp.where(seq == 0, came, kept)], axis=0
    )
    far = moved(heads, by_two)
    blocks = [heads, far, moved(heads, pair), moved(far, pair)]
    per = heads.shape[0]
    added = []
    for cols in out_cols:
        total = 0.0
        for p, block in enumerate(blocks):
            total = total + jnp.dot(
                cols[:, p * per : (p + 1) * per], block, preferred_element_type=f32
            )
        added.append(total)
    total = residual.astype(f32) + jnp.concatenate([half[:part] for half in added], axis=0)
    for r in range(1, 4):
        share = jnp.concatenate(
            [half[r * part : (r + 1) * part].astype(bf16) for half in added], axis=0
        )
        total = total + moved(share, lambda y, x, c, r=r: (y, (x - r) % 4, c)).astype(f32)
    result = total.astype(bf16)

    own, away = result[:part], moved(result[part:], other_core)
    handed_on = jnp.concatenate(
        [jnp.where(core == 0, own, away), jnp.where(core == 0, away, own)], axis=1
    )
    return handed_on.T[None]


def solution(mesh):
    fine = Mesh(mesh.devices.reshape(8, 4, 4, 2, 2), ("section", "yl", "x", "core", "seq"))
    placed = (
        P("section", "seq", DP),
        P("section", DP),
        P("section", "seq", DP),
        P("section", None, DP),
        P("section", "seq", None),
        P("section", None),
    )
    return jax.shard_map(
        shards, mesh=fine, in_specs=placed, out_specs=P("section", "seq", DP), check_vma=False
    )
```

```python
import math

import jax
import jax.numpy as jnp
from jax import lax
from jax.experimental import pallas as pl
from jax.experimental.pallas import tpu as pltpu
from jax.sharding import Mesh, PartitionSpec as P

BLOCK = 64
PLANE = ("yl", "x", "core", "seq")
DP = ("yl", "x", "core")
NEG = -1e30


def pairs_of(where):
    pairs = []
    for yl in range(4):
        for x in range(4):
            for core in range(2):
                for seq in range(2):
                    target = where(seq * 4 + yl, x, core)
                    if target is None:
                        continue
                    ty, tx, tc = target
                    source_at = ((yl * 4 + x) * 2 + core) * 2 + seq
                    target_at = (((ty % 4) * 4 + tx) * 2 + tc) * 2 + ty // 4
                    pairs.append((source_at, target_at))
    return pairs


def moved(value, where):
    return lax.ppermute(value, PLANE, pairs_of(where))


def moved_on(value, where):
    sections, plane = lax.axis_size("section"), 64
    pairs = [
        (i * plane + a, (i + 1) % sections * plane + b)
        for i in range(sections)
        for a, b in pairs_of(where)
    ]
    return lax.ppermute(value, ("section", *PLANE), pairs)


def swap_inner(y, x, core):
    if y in (2, 3):
        return y + 2, x, core
    if y in (4, 5):
        return y - 2, x, core
    return y, x, core


def other_seq(y, x, core):
    return (y + 4) % 8, x, core


def block_mask(query_ids, random_rows, global_ids, key_ids):
    query_col = query_ids[:, None]
    key_ids = key_ids[None, :]
    adjacent = jnp.abs(query_col - key_ids) <= 1
    key_global = jnp.any(key_ids[:, :, None] == global_ids[None, None, :], axis=2)
    query_global = jnp.any(query_col[:, :, None] == global_ids[None, None, :], axis=2)
    chosen = jnp.any(random_rows[:, None, :] == key_ids[:, :, None], axis=2)
    return adjacent | key_global | query_global | chosen


def attention_kernel(scale, per, flag_ref, *refs):
    own_refs, other_refs = refs[:2], refs[2:4]
    bias_ref, sent_ref, kept_ref, rows_ref, value_ref, wide_ref = refs[4:]
    size, tile = sent_ref.shape
    at = pl.program_id(0)

    @pl.when(at == 0)
    def _():
        step = per * tile
        for i in range(2):
            here, there = pl.ds(i * step, step), pl.ds((2 + i) * step, step)
            rows_ref[here, :size] = own_refs[i][size : 2 * size, :].T
            rows_ref[there, :size] = other_refs[i][:size, :].T
            value_ref[:, here] = own_refs[i][2 * size :, :]
            value_ref[:, there] = other_refs[i][size:, :]
        shape = (rows_ref.shape[0], size)
        block = lax.broadcasted_iota(jnp.int32, shape, 0) // BLOCK
        column = lax.broadcasted_iota(jnp.int32, shape, 1)
        rows_ref[:, size:] = jnp.where(block == column, 1.0, 0.0).astype(jnp.bfloat16)
        wide_ref[...] = jnp.zeros_like(wide_ref)

    columns = pl.ds(pl.multiple_of(lax.rem(at, per) * tile, tile), tile)
    use_f = (at < per) == (flag_ref[0] > 0)

    @pl.when(use_f)
    def _():
        wide_ref[:size, :] = own_refs[1][:size, columns]

    @pl.when(jnp.logical_not(use_f))
    def _():
        wide_ref[:size, :] = own_refs[0][:size, columns]

    wide_ref[size : size + bias_ref.shape[0], :] = bias_ref[...]
    scores = jnp.dot(rows_ref[...], wide_ref[...], preferred_element_type=jnp.float32)
    highest = jnp.max(scores, axis=0, keepdims=True)
    weights = jnp.exp((scores - highest) * scale)
    totals = jnp.sum(weights, axis=0, keepdims=True)
    mixed = jnp.dot(
        value_ref[...], weights.astype(jnp.bfloat16), preferred_element_type=jnp.float32
    )
    mixed = (mixed / totals).astype(jnp.bfloat16)

    @pl.when(at < per)
    def _():
        sent_ref[...] = mixed

    @pl.when(at >= per)
    def _():
        kept_ref[...] = mixed


def attention(flag, own, other, bias):
    triple, step = own[0].shape
    size, tile = triple // 3, 256
    per = step // tile

    def whole(array):
        return pl.BlockSpec(array.shape, lambda i, flag: (0, 0))

    return pl.pallas_call(
        lambda *refs: attention_kernel(1.0 / math.sqrt(size), per, *refs),
        grid_spec=pltpu.PrefetchScalarGridSpec(
            num_scalar_prefetch=1,
            grid=(2 * per,),
            in_specs=[whole(array) for array in (*own, *other)]
            + [pl.BlockSpec((bias.shape[0], tile), lambda i, flag: (0, i))],
            out_specs=[
                pl.BlockSpec((size, tile), lambda i, flag: (0, jnp.minimum(i, per - 1))),
                pl.BlockSpec((size, tile), lambda i, flag: (0, jnp.maximum(i - per, 0))),
            ],
            scratch_shapes=[
                pltpu.VMEM((4 * step, 2 * size), jnp.bfloat16),
                pltpu.VMEM((size, 4 * step), jnp.bfloat16),
                pltpu.VMEM((2 * size, tile), jnp.bfloat16),
            ],
        ),
        out_shape=[jax.ShapeDtypeStruct((size, step), jnp.bfloat16)] * 2,
        cost_estimate=pl.CostEstimate(
            flops=32 * size * step * step, bytes_accessed=12 * size * step, transcendentals=8 * step * step
        ),
        name="attention",
    )(flag, *own, *other, bias)


def slices_kernel(order_ref, ring_ref, source_ref, *out_refs):
    for r, out_ref in enumerate(out_refs):
        per = out_ref.shape[1]
        start = pl.multiple_of(ring_ref[r] * per, per)
        out_ref[...] = source_ref[:, pl.ds(start, per)]


def column_slices(matrix, order, ring):
    rows, width = matrix.shape
    block = pl.BlockSpec((rows, width // 16), lambda p, order, ring: (0, p))
    return pl.pallas_call(
        slices_kernel,
        grid_spec=pltpu.PrefetchScalarGridSpec(
            num_scalar_prefetch=2,
            grid=(4,),
            in_specs=[pl.BlockSpec((rows, width // 4), lambda p, order, ring: (0, order[p]))],
            out_specs=[block] * 4,
        ),
        out_shape=[jax.ShapeDtypeStruct((rows, width // 4), matrix.dtype)] * 4,
        cost_estimate=pl.CostEstimate(
            flops=0, bytes_accessed=4 * rows * width, transcendentals=0
        ),
        name="column_slices",
    )(order, ring, matrix)


def rows_kernel(*refs):
    *parts, out_ref = refs
    start = 0
    for part in parts:
        out_ref[start : start + part.shape[0], :] = part[...]
        start += part.shape[0]


def stacked_rows(*parts):
    rows = sum(part.shape[0] for part in parts)
    vmem = pl.BlockSpec(memory_space=pltpu.VMEM)
    return pl.pallas_call(
        rows_kernel,
        in_specs=[vmem] * len(parts),
        out_specs=vmem,
        out_shape=jax.ShapeDtypeStruct((rows, parts[0].shape[1]), parts[0].dtype),
        cost_estimate=pl.CostEstimate(
            flops=0, bytes_accessed=4 * rows * parts[0].shape[1], transcendentals=0
        ),
        name="stacked_rows",
    )(*parts)


def after(value, earlier):
    return lax.optimization_barrier((value, earlier))[0]


def at_index(array, index, axis=0):
    return lax.dynamic_index_in_dim(array, index, axis=axis, keepdims=False)


def other_core(y, x, core):
    return y, x, 1 - core


def pair(y, x, core):
    return y ^ 1, x, core


def by_two(y, x, core):
    return y ^ 2, x, core


def around(y, x, core):
    return y, (x + 1 - 2 * core) % 4, core


def same(y, x, core):
    return y, x, core


def shards(section_input, norm_gain, qkv_weight, out_weight, random_blocks, global_blocks):
    yl, x, core, seq = (lax.axis_index(axis) for axis in PLANE)
    f32, bf16 = jnp.float32, jnp.bfloat16
    tokens_t = section_input[0].T
    part, length = tokens_t.shape
    step = length // 2
    width = part * 32
    first = yl // 2

    def of_core(array):
        halves = array[:, :step], array[:, step:]
        return jnp.where(core == 0, *halves), jnp.where(core == 0, *halves[::-1])

    own, away = of_core(tokens_t)
    crossed = moved(away, lambda *at: other_core(*swap_inner(*at)))
    e = stacked_rows(moved(own, swap_inner), crossed)
    out_next = moved_on(out_weight[0].T, same)

    gain = norm_gain
    gain_row = jnp.pad(gain, ((0, 15), (0, step - part)))
    beside = moved(jnp.concatenate([away, gain_row], axis=0), other_core)
    gain = jnp.concatenate([gain, beside[part : part + 1, :part]], axis=1).astype(f32)
    item = jnp.concatenate([own, beside[:part]], axis=0)
    as_float = item.astype(f32)
    squares = jnp.sum(as_float * as_float, axis=0)
    random = random_blocks[0]
    numbers = jnp.pad(random.astype(f32).reshape(-1), (0, step - random.size))
    mine = jnp.stack([squares, numbers])
    theirs = moved(mine, other_seq)
    random = jnp.stack([theirs[1, : random.size].astype(jnp.int32).reshape(random.shape), random])
    slot = (yl * 4 + x == jnp.arange(16))[:, None]
    table = jnp.where(slot, jnp.pad(gain, ((0, 0), (0, step - 2 * part))), 0.0)
    table = jnp.concatenate([table, mine[:1], theirs[:1]], axis=0)
    table = table + moved(table, lambda y, x, c: (y, x ^ 1, c))
    e = after(e, table)
    f = moved(e, by_two)
    e_pair = moved(e, pair)
    e_ring = [e]
    for _ in range(3):
        e_ring.append(moved(e_ring[-1], around))
    f = after(f, e_ring[1])
    e_pair = after(e_pair, e_ring[2])
    f_two = after(stacked_rows(f, moved(f, pair)), e_ring[3])
    pair_ring = [e_pair]
    for _ in range(3):
        pair_ring.append(moved(pair_ring[-1], around))
    table = after(table, pair_ring[1])
    for where in (lambda y, x, c: (y, x ^ 2, c), pair, by_two):
        table = table + moved(table, where)
    factors = lax.rsqrt(table[16:] / width + 1e-05)
    factor_e = jnp.where(first == seq, factors[:1], factors[1:])
    factor_f = jnp.where(first == seq, factors[1:], factors[:1])
    gains = table[:16, : 2 * part].reshape(2, 2, 4, 2 * part)
    gains = at_index(gains, seq)

    weight = after(qkv_weight[0], e_pair)
    beside = moved(weight, other_core)
    columns = weight.shape[1]
    weight = jnp.concatenate(
        [jnp.where(core == seq, weight, beside), jnp.where(core == seq, beside, weight)], axis=1
    )
    weight = weight.reshape(2, 4, 2, part, 2 * columns)
    weights, scales = [], []
    for k in range(4):
        source = (x - (1 - 2 * core) * k) % 4
        weights.append([])
        scales.append([])
        for ab in range(2):
            which = ab ^ (yl % 2)
            block = at_index(at_index(weight, which), source)
            weights[k].append(
                jnp.concatenate([at_index(block, core), at_index(block, 1 - core)], axis=0)
            )
            scales[k].append(at_index(at_index(gains, which), source))

    def project(block, k, which, factor):
        rows = jnp.concatenate([weights[k][ab] for ab in which], axis=0)
        scale = jnp.concatenate([scales[k][ab] for ab in which]).reshape(-1, 1)
        normed = (block.astype(f32) * factor * scale).astype(bf16)
        return lax.dot_general(
            rows, normed, (((0,), (0,)), ((), ())), preferred_element_type=f32
        )

    count = step // BLOCK
    rows = lax.dynamic_slice_in_dim(random, core * count, count, axis=1).reshape(2 * count, -1)
    spot = jnp.arange(count, dtype=jnp.int32)

    def block_ids(halves, core):
        halves = jnp.stack(halves) * 2 * count
        return (halves[:, None] + core * count + spot[None, :]).reshape(-1)

    query_ids = block_ids([1 - seq, seq], core)
    key_ids = jnp.concatenate(
        [block_ids([first, 1 - first], core), block_ids([first, 1 - first], 1 - core)]
    )
    allowed = block_mask(query_ids, rows, global_blocks[0], key_ids)
    bias = jnp.repeat(jnp.where(allowed.T, 0.0, NEG), BLOCK, axis=1).astype(bf16)

    f = f_two
    partial_e = project(e, 0, (0,), factor_e) + project(e_pair, 0, (1,), factor_e)
    partial_f = project(f, 0, (0, 1), factor_f)
    for k in range(1, 4):
        f = moved(f, around)
        partial_e = partial_e + project(e_ring[k], k, (0,), factor_e)
        partial_e = partial_e + project(pair_ring[k], k, (1,), factor_e)
        partial_f = partial_f + project(f, k, (0, 1), factor_f)
    order = after(jnp.stack([yl, yl ^ 2, yl ^ 1, yl ^ 3]), f_two)
    ring = (x + jnp.arange(4, dtype=jnp.int32)) % 4
    slices = column_slices(out_next, order, ring)
    sends = [partial[columns:].astype(bf16) for partial in (partial_e, partial_f)]
    sends[0], slices = lax.optimization_barrier((sends[0], slices))
    residual = moved_on(after(item, sends[1]), same)
    out_own = [slices[0]]
    for r in range(1, 4):
        out_own.append(moved(slices[r], lambda y, x, c, r=r: (y, (x + r) % 4, c)))
    joined, other = [], []
    head = columns // 3
    for partial, send in zip((partial_e, partial_f), sends):
        came = after(moved(send, other_seq), other)
        joined.append((partial[:columns] + came.astype(f32)).astype(bf16))
        other.append(moved(joined[-1][head:], other_core))

    flag = after((first == seq).astype(jnp.int32).reshape(1), (out_own, residual))
    out_own = stacked_rows(*out_own)
    out_cols = out_own, moved(out_own, other_core)
    sent, kept = attention(flag, joined, other, bias)
    came, kept = moved_on(sent, other_seq), moved_on(kept, same)

    heads = jnp.concatenate(
        [jnp.where(seq == 0, kept, came), jnp.where(seq == 0, came, kept)], axis=0
    )
    far = moved(heads, by_two)
    blocks = [heads, far, moved(heads, pair), moved(far, pair)]
    per = heads.shape[0]
    added = []
    for cols in out_cols:
        total = 0.0
        for p, block in enumerate(blocks):
            total = total + jnp.dot(
                cols[:, p * per : (p + 1) * per], block, preferred_element_type=f32
            )
        added.append(total)
    total = residual.astype(f32) + jnp.concatenate([half[:part] for half in added], axis=0)
    for r in range(1, 4):
        share = jnp.concatenate(
            [half[r * part : (r + 1) * part].astype(bf16) for half in added], axis=0
        )
        total = total + moved(share, lambda y, x, c, r=r: (y, (x - r) % 4, c)).astype(f32)
    result = total.astype(bf16)

    own, away = result[:part], moved(result[part:], other_core)
    handed_on = jnp.concatenate(
        [jnp.where(core == 0, own, away), jnp.where(core == 0, away, own)], axis=1
    )
    return handed_on.T[None]


def solution(mesh):
    fine = Mesh(mesh.devices.reshape(8, 4, 4, 2, 2), ("section", "yl", "x", "core", "seq"))
    placed = (
        P("section", "seq", DP),
        P("section", DP),
        P("section", "seq", DP),
        P("section", None, DP),
        P("section", "seq", None),
        P("section", None),
    )
    return jax.shard_map(
        shards, mesh=fine, in_specs=placed, out_specs=P("section", "seq", DP), check_vma=False
    )
```

```python
import math

import jax
import jax.numpy as jnp
from jax import lax
from jax.experimental import pallas as pl
from jax.experimental.pallas import tpu as pltpu
from jax.sharding import Mesh, PartitionSpec as P

BLOCK = 64
PLANE = ("yl", "x", "core", "seq")
DP = ("yl", "x", "core")
NEG = -1e30


def pairs_of(where):
    pairs = []
    for yl in range(4):
        for x in range(4):
            for core in range(2):
                for seq in range(2):
                    target = where(seq * 4 + yl, x, core)
                    if target is None:
                        continue
                    ty, tx, tc = target
                    source_at = ((yl * 4 + x) * 2 + core) * 2 + seq
                    target_at = (((ty % 4) * 4 + tx) * 2 + tc) * 2 + ty // 4
                    pairs.append((source_at, target_at))
    return pairs


def moved(value, where):
    return lax.ppermute(value, PLANE, pairs_of(where))


def moved_on(value, where):
    sections, plane = lax.axis_size("section"), 64
    pairs = [
        (i * plane + a, (i + 1) % sections * plane + b)
        for i in range(sections)
        for a, b in pairs_of(where)
    ]
    return lax.ppermute(value, ("section", *PLANE), pairs)


def swap_inner(y, x, core):
    if y in (2, 3):
        return y + 2, x, core
    if y in (4, 5):
        return y - 2, x, core
    return y, x, core


def other_seq(y, x, core):
    return (y + 4) % 8, x, core


def block_mask(query_ids, random_rows, global_ids, key_ids):
    query_col = query_ids[:, None]
    key_ids = key_ids[None, :]
    adjacent = jnp.abs(query_col - key_ids) <= 1
    key_global = jnp.any(key_ids[:, :, None] == global_ids[None, None, :], axis=2)
    query_global = jnp.any(query_col[:, :, None] == global_ids[None, None, :], axis=2)
    chosen = jnp.any(random_rows[:, None, :] == key_ids[:, :, None], axis=2)
    return adjacent | key_global | query_global | chosen


def attention_kernel(scale, per, flag_ref, *refs):
    own_refs, other_refs = refs[:2], refs[2:4]
    bias_ref, sent_ref, kept_ref, rows_ref, value_ref, wide_ref = refs[4:]
    size, tile = sent_ref.shape
    at = pl.program_id(0)

    @pl.when(at == 0)
    def _():
        step = per * tile
        for i in range(2):
            here, there = pl.ds(i * step, step), pl.ds((2 + i) * step, step)
            rows_ref[here, :size] = own_refs[i][size : 2 * size, :].T
            rows_ref[there, :size] = other_refs[i][:size, :].T
            value_ref[:, here] = own_refs[i][2 * size :, :]
            value_ref[:, there] = other_refs[i][size:, :]
        shape = (rows_ref.shape[0], size)
        block = lax.broadcasted_iota(jnp.int32, shape, 0) // BLOCK
        column = lax.broadcasted_iota(jnp.int32, shape, 1)
        rows_ref[:, size:] = jnp.where(block == column, 1.0, 0.0).astype(jnp.bfloat16)
        wide_ref[...] = jnp.zeros_like(wide_ref)

    columns = pl.ds(pl.multiple_of(lax.rem(at, per) * tile, tile), tile)
    use_f = (at < per) == (flag_ref[0] > 0)

    @pl.when(use_f)
    def _():
        wide_ref[:size, :] = own_refs[1][:size, columns]

    @pl.when(jnp.logical_not(use_f))
    def _():
        wide_ref[:size, :] = own_refs[0][:size, columns]

    wide_ref[size : size + bias_ref.shape[0], :] = bias_ref[...]
    scores = jnp.dot(rows_ref[...], wide_ref[...], preferred_element_type=jnp.float32)
    highest = jnp.max(scores, axis=0, keepdims=True)
    weights = jnp.exp((scores - highest) * scale)
    totals = jnp.sum(weights, axis=0, keepdims=True)
    mixed = jnp.dot(
        value_ref[...], weights.astype(jnp.bfloat16), preferred_element_type=jnp.float32
    )
    mixed = (mixed / totals).astype(jnp.bfloat16)

    @pl.when(at < per)
    def _():
        sent_ref[...] = mixed

    @pl.when(at >= per)
    def _():
        kept_ref[...] = mixed


def attention(flag, own, other, bias):
    triple, step = own[0].shape
    size, tile = triple // 3, 256
    per = step // tile

    def whole(array):
        return pl.BlockSpec(array.shape, lambda i, flag: (0, 0))

    return pl.pallas_call(
        lambda *refs: attention_kernel(1.0 / math.sqrt(size), per, *refs),
        grid_spec=pltpu.PrefetchScalarGridSpec(
            num_scalar_prefetch=1,
            grid=(2 * per,),
            in_specs=[whole(array) for array in (*own, *other)]
            + [pl.BlockSpec((bias.shape[0], tile), lambda i, flag: (0, i))],
            out_specs=[
                pl.BlockSpec((size, tile), lambda i, flag: (0, jnp.minimum(i, per - 1))),
                pl.BlockSpec((size, tile), lambda i, flag: (0, jnp.maximum(i - per, 0))),
            ],
            scratch_shapes=[
                pltpu.VMEM((4 * step, 2 * size), jnp.bfloat16),
                pltpu.VMEM((size, 4 * step), jnp.bfloat16),
                pltpu.VMEM((2 * size, tile), jnp.bfloat16),
            ],
        ),
        out_shape=[jax.ShapeDtypeStruct((size, step), jnp.bfloat16)] * 2,
        cost_estimate=pl.CostEstimate(
            flops=32 * size * step * step, bytes_accessed=12 * size * step, transcendentals=8 * step * step
        ),
        name="attention",
    )(flag, *own, *other, bias)


def slices_kernel(order_ref, ring_ref, source_ref, *out_refs):
    for r, out_ref in enumerate(out_refs):
        per = out_ref.shape[1]
        start = pl.multiple_of(ring_ref[r] * per, per)
        out_ref[...] = source_ref[:, pl.ds(start, per)]


def column_slices(matrix, order, ring, width):
    rows = matrix.shape[0]
    block = pl.BlockSpec((rows, width // 16), lambda p, order, ring: (0, p))
    return pl.pallas_call(
        slices_kernel,
        grid_spec=pltpu.PrefetchScalarGridSpec(
            num_scalar_prefetch=2,
            grid=(4,),
            in_specs=[pl.BlockSpec((rows, width // 4), lambda p, order, ring: (0, order[p]))],
            out_specs=[block] * 4,
        ),
        out_shape=[jax.ShapeDtypeStruct((rows, width // 4), matrix.dtype)] * 4,
        cost_estimate=pl.CostEstimate(
            flops=0, bytes_accessed=4 * rows * width, transcendentals=0
        ),
        name="column_slices",
    )(order, ring, matrix)


def rows_kernel(*refs):
    *parts, out_ref = refs
    start = 0
    for part in parts:
        out_ref[start : start + part.shape[0], :] = part[...]
        start += part.shape[0]


def stacked_rows(*parts):
    rows = sum(part.shape[0] for part in parts)
    vmem = pl.BlockSpec(memory_space=pltpu.VMEM)
    return pl.pallas_call(
        rows_kernel,
        in_specs=[vmem] * len(parts),
        out_specs=vmem,
        out_shape=jax.ShapeDtypeStruct((rows, parts[0].shape[1]), parts[0].dtype),
        cost_estimate=pl.CostEstimate(
            flops=0, bytes_accessed=4 * rows * parts[0].shape[1], transcendentals=0
        ),
        name="stacked_rows",
    )(*parts)


def after(value, earlier):
    return lax.optimization_barrier((value, earlier))[0]


def at_index(array, index, axis=0):
    return lax.dynamic_index_in_dim(array, index, axis=axis, keepdims=False)


def other_core(y, x, core):
    return y, x, 1 - core


def pair(y, x, core):
    return y ^ 1, x, core


def by_two(y, x, core):
    return y ^ 2, x, core


def around(y, x, core):
    return y, (x + 1 - 2 * core) % 4, core


def same(y, x, core):
    return y, x, core


def shards(section_input, norm_gain, qkv_weight, out_weight, random_blocks, global_blocks):
    yl, x, core, seq = (lax.axis_index(axis) for axis in PLANE)
    f32, bf16 = jnp.float32, jnp.bfloat16
    tokens_t = section_input[0].T
    part, length = tokens_t.shape
    step = length // 2
    width = part * 32
    first = yl // 2

    def of_core(array):
        halves = array[:, :step], array[:, step:]
        return jnp.where(core == 0, *halves), jnp.where(core == 0, *halves[::-1])

    own, away = of_core(tokens_t)
    crossed = moved(away, lambda *at: other_core(*swap_inner(*at)))
    e = stacked_rows(moved(own, swap_inner), crossed)
    gain = norm_gain
    gain_row = jnp.pad(gain, ((0, 15), (0, step - part)))
    beside = moved(jnp.concatenate([away, gain_row], axis=0), other_core)
    gain = jnp.concatenate([gain, beside[part : part + 1, :part]], axis=1).astype(f32)
    item = jnp.concatenate([own, beside[:part]], axis=0)
    as_float = item.astype(f32)
    squares = jnp.sum(as_float * as_float, axis=0)
    ahead = moved_on(out_weight[0].T, same)
    random = random_blocks[0]
    numbers = jnp.pad(random.astype(f32).reshape(-1), (0, step - random.size))
    mine = jnp.stack([squares, numbers])
    theirs = moved(mine, other_seq)
    random = jnp.stack([theirs[1, : random.size].astype(jnp.int32).reshape(random.shape), random])
    slot = (yl * 4 + x == jnp.arange(16))[:, None]
    table = jnp.where(slot, jnp.pad(gain, ((0, 0), (0, step - 2 * part))), 0.0)
    table = jnp.concatenate([table, mine[:1], theirs[:1]], axis=0)
    table = table + moved(table, lambda y, x, c: (y, x ^ 1, c))
    e = after(e, table)
    f = moved(e, by_two)
    table = table + moved(table, lambda y, x, c: (y, x ^ 2, c))
    e_two = stacked_rows(e, after(moved(e, pair), (table, f)))
    f_pair = moved(f, pair)
    table = table + moved(table, pair)
    e_next = moved(e_two, around)
    f_two = after(stacked_rows(f, after(f_pair, table)), e_next)
    table = table + moved(table, by_two)
    e_ring, f_ring = [e_two, e_next], [f_two, moved(f_two, around)]
    f_ring[1] = after(f_ring[1], table)
    for _ in range(2):
        e_ring.append(moved(e_ring[-1], around))
        f_ring.append(moved(f_ring[-1], around))
    factors = lax.rsqrt(table[16:] / width + 1e-05)
    factor_e = jnp.where(first == seq, factors[:1], factors[1:])
    factor_f = jnp.where(first == seq, factors[1:], factors[:1])
    gains = table[:16, : 2 * part].reshape(2, 2, 4, 2 * part)
    gains = at_index(gains, seq)

    weight = after(qkv_weight[0], theirs)
    beside = moved(weight, other_core)
    columns = weight.shape[1]
    weight = jnp.concatenate(
        [jnp.where(core == seq, weight, beside), jnp.where(core == seq, beside, weight)], axis=1
    )
    weight = weight.reshape(2, 4, 2, part, 2 * columns)
    weights, scales = [], []
    for k in range(4):
        source = (x - (1 - 2 * core) * k) % 4
        rows, scale = [], []
        for ab in range(2):
            which = ab ^ (yl % 2)
            block = at_index(at_index(weight, which), source)
            rows += [at_index(block, core), at_index(block, 1 - core)]
            scale.append(at_index(at_index(gains, which), source))
        weights.append(jnp.concatenate(rows, axis=0).T)
        scales.append(jnp.concatenate(scale).reshape(4 * part, 1))

    def project(block, k, factor):
        normed = (block.astype(f32) * factor * scales[k]).astype(bf16)
        return jnp.dot(weights[k], normed, preferred_element_type=f32)

    count = step // BLOCK
    rows = lax.dynamic_slice_in_dim(random, core * count, count, axis=1).reshape(2 * count, -1)
    spot = jnp.arange(count, dtype=jnp.int32)

    def block_ids(halves, core):
        halves = jnp.stack(halves) * 2 * count
        return (halves[:, None] + core * count + spot[None, :]).reshape(-1)

    query_ids = block_ids([1 - seq, seq], core)
    key_ids = jnp.concatenate(
        [block_ids([first, 1 - first], core), block_ids([first, 1 - first], 1 - core)]
    )
    allowed = block_mask(query_ids, rows, global_blocks[0], key_ids)
    bias = jnp.repeat(jnp.where(allowed.T, 0.0, NEG), BLOCK, axis=1).astype(bf16)

    partial_e = partial_f = 0.0
    for k in range(4):
        partial_e = partial_e + project(e_ring[k], k, factor_e)
        partial_f = partial_f + project(f_ring[k], k, factor_f)
    order = after(jnp.stack([yl, yl ^ 2, yl ^ 1, yl ^ 3]), f_two)
    ring = (x + jnp.arange(4, dtype=jnp.int32)) % 4
    slices = column_slices(ahead, order, ring, out_weight.shape[1])
    sends = [partial[columns:].astype(bf16) for partial in (partial_e, partial_f)]
    sends[0], slices = lax.optimization_barrier((sends[0], slices))
    out_own = [slices[0]]
    for r in range(1, 4):
        out_own.append(moved(slices[r], lambda y, x, c, r=r: (y, (x + r) % 4, c)))
    joined, other = [], []
    head = columns // 3
    for partial, send in zip((partial_e, partial_f), sends):
        came = after(moved(send, other_seq), (other, sends[1]))
        joined.append((partial[:columns] + came.astype(f32)).astype(bf16))
        other.append(moved(joined[-1][head:], other_core))

    flag = after((first == seq).astype(jnp.int32).reshape(1), out_own)
    out_own = stacked_rows(*out_own)
    out_cols = out_own, moved(out_own, other_core)
    sent, kept = attention(flag, joined, other, bias)
    came, kept = moved_on(sent, other_seq), moved_on(kept, same)
    residual = moved_on(after(item, sent), same)

    heads = jnp.concatenate(
        [jnp.where(seq == 0, kept, came), jnp.where(seq == 0, came, kept)], axis=0
    )
    far = moved(heads, by_two)
    blocks = [heads, far, moved(heads, pair), moved(far, pair)]
    per = heads.shape[0]
    added = []
    for cols in out_cols:
        total = 0.0
        for p, block in enumerate(blocks):
            total = total + jnp.dot(
                cols[:, p * per : (p + 1) * per], block, preferred_element_type=f32
            )
        added.append(total)
    total = residual.astype(f32) + jnp.concatenate([half[:part] for half in added], axis=0)
    for r in range(1, 4):
        share = jnp.concatenate(
            [half[r * part : (r + 1) * part].astype(bf16) for half in added], axis=0
        )
        total = total + moved(share, lambda y, x, c, r=r: (y, (x - r) % 4, c)).astype(f32)
    result = total.astype(bf16)

    own, away = result[:part], moved(result[part:], other_core)
    handed_on = jnp.concatenate(
        [jnp.where(core == 0, own, away), jnp.where(core == 0, away, own)], axis=1
    )
    return handed_on.T[None]


def solution(mesh):
    fine = Mesh(mesh.devices.reshape(8, 4, 4, 2, 2), ("section", "yl", "x", "core", "seq"))
    placed = (
        P("section", "seq", DP),
        P("section", DP),
        P("section", "seq", DP),
        P("section", None, DP),
        P("section", "seq", None),
        P("section", None),
    )
    return jax.shard_map(
        shards, mesh=fine, in_specs=placed, out_specs=P("section", "seq", DP), check_vma=False
    )
```

```python
import math

import jax
import jax.numpy as jnp
from jax import lax
from jax.experimental import pallas as pl
from jax.experimental.pallas import tpu as pltpu
from jax.sharding import Mesh, PartitionSpec as P

BLOCK = 64
PLANE = ("yl", "x", "core", "seq")
DP = ("yl", "x", "core")
NEG = -1e30


def pairs_of(where):
    pairs = []
    for yl in range(4):
        for x in range(4):
            for core in range(2):
                for seq in range(2):
                    target = where(seq * 4 + yl, x, core)
                    if target is None:
                        continue
                    ty, tx, tc = target
                    source_at = ((yl * 4 + x) * 2 + core) * 2 + seq
                    target_at = (((ty % 4) * 4 + tx) * 2 + tc) * 2 + ty // 4
                    pairs.append((source_at, target_at))
    return pairs


def moved(value, where):
    return lax.ppermute(value, PLANE, pairs_of(where))


def moved_on(value, where):
    sections, plane = lax.axis_size("section"), 64
    pairs = [
        (i * plane + a, (i + 1) % sections * plane + b)
        for i in range(sections)
        for a, b in pairs_of(where)
    ]
    return lax.ppermute(value, ("section", *PLANE), pairs)


def swap_inner(y, x, core):
    if y in (2, 3):
        return y + 2, x, core
    if y in (4, 5):
        return y - 2, x, core
    return y, x, core


def other_seq(y, x, core):
    return (y + 4) % 8, x, core


def block_mask(query_ids, random_rows, global_ids, key_ids):
    query_col = query_ids[:, None]
    key_ids = key_ids[None, :]
    adjacent = jnp.abs(query_col - key_ids) <= 1
    key_global = jnp.any(key_ids[:, :, None] == global_ids[None, None, :], axis=2)
    query_global = jnp.any(query_col[:, :, None] == global_ids[None, None, :], axis=2)
    chosen = jnp.any(random_rows[:, None, :] == key_ids[:, :, None], axis=2)
    return adjacent | key_global | query_global | chosen


def attention_kernel(scale, per, flag_ref, *refs):
    own_refs, other_refs = refs[:2], refs[2:4]
    bias_ref, sent_ref, kept_ref, rows_ref, value_ref, wide_ref = refs[4:]
    size, tile = sent_ref.shape
    at = pl.program_id(0)

    @pl.when(at == 0)
    def _():
        step = per * tile
        for i in range(2):
            here, there = pl.ds(i * step, step), pl.ds((2 + i) * step, step)
            rows_ref[here, :size] = own_refs[i][size : 2 * size, :].T
            rows_ref[there, :size] = other_refs[i][:size, :].T
            value_ref[:, here] = own_refs[i][2 * size :, :]
            value_ref[:, there] = other_refs[i][size:, :]
        shape = (rows_ref.shape[0], size)
        block = lax.broadcasted_iota(jnp.int32, shape, 0) // BLOCK
        column = lax.broadcasted_iota(jnp.int32, shape, 1)
        rows_ref[:, size:] = jnp.where(block == column, 1.0, 0.0).astype(jnp.bfloat16)
        wide_ref[...] = jnp.zeros_like(wide_ref)

    columns = pl.ds(pl.multiple_of(lax.rem(at, per) * tile, tile), tile)
    use_f = (at < per) == (flag_ref[0] > 0)

    @pl.when(use_f)
    def _():
        wide_ref[:size, :] = own_refs[1][:size, columns]

    @pl.when(jnp.logical_not(use_f))
    def _():
        wide_ref[:size, :] = own_refs[0][:size, columns]

    wide_ref[size : size + bias_ref.shape[0], :] = bias_ref[...]
    scores = jnp.dot(rows_ref[...], wide_ref[...], preferred_element_type=jnp.float32)
    highest = jnp.max(scores, axis=0, keepdims=True)
    weights = jnp.exp((scores - highest) * scale)
    totals = jnp.sum(weights, axis=0, keepdims=True)
    mixed = jnp.dot(
        value_ref[...], weights.astype(jnp.bfloat16), preferred_element_type=jnp.float32
    )
    mixed = (mixed / totals).astype(jnp.bfloat16)

    @pl.when(at < per)
    def _():
        sent_ref[...] = mixed

    @pl.when(at >= per)
    def _():
        kept_ref[...] = mixed


def attention(flag, own, other, bias):
    triple, step = own[0].shape
    size, tile = triple // 3, 256
    per = step // tile

    def whole(array):
        return pl.BlockSpec(array.shape, lambda i, flag: (0, 0))

    return pl.pallas_call(
        lambda *refs: attention_kernel(1.0 / math.sqrt(size), per, *refs),
        grid_spec=pltpu.PrefetchScalarGridSpec(
            num_scalar_prefetch=1,
            grid=(2 * per,),
            in_specs=[whole(array) for array in (*own, *other)]
            + [pl.BlockSpec((bias.shape[0], tile), lambda i, flag: (0, i))],
            out_specs=[
                pl.BlockSpec((size, tile), lambda i, flag: (0, jnp.minimum(i, per - 1))),
                pl.BlockSpec((size, tile), lambda i, flag: (0, jnp.maximum(i - per, 0))),
            ],
            scratch_shapes=[
                pltpu.VMEM((4 * step, 2 * size), jnp.bfloat16),
                pltpu.VMEM((size, 4 * step), jnp.bfloat16),
                pltpu.VMEM((2 * size, tile), jnp.bfloat16),
            ],
        ),
        out_shape=[jax.ShapeDtypeStruct((size, step), jnp.bfloat16)] * 2,
        cost_estimate=pl.CostEstimate(
            flops=32 * size * step * step, bytes_accessed=12 * size * step, transcendentals=8 * step * step
        ),
        name="attention",
    )(flag, *own, *other, bias)


def slices_kernel(order_ref, ring_ref, source_ref, *out_refs):
    for r, out_ref in enumerate(out_refs):
        per = out_ref.shape[1]
        start = pl.multiple_of(ring_ref[r] * per, per)
        out_ref[...] = source_ref[:, pl.ds(start, per)]


def column_slices(matrix, order, ring):
    rows, width = matrix.shape
    block = pl.BlockSpec((rows, width // 16), lambda p, order, ring: (0, p))
    return pl.pallas_call(
        slices_kernel,
        grid_spec=pltpu.PrefetchScalarGridSpec(
            num_scalar_prefetch=2,
            grid=(4,),
            in_specs=[pl.BlockSpec((rows, width // 4), lambda p, order, ring: (0, order[p]))],
            out_specs=[block] * 4,
        ),
        out_shape=[jax.ShapeDtypeStruct((rows, width // 4), matrix.dtype)] * 4,
        cost_estimate=pl.CostEstimate(
            flops=0, bytes_accessed=4 * rows * width, transcendentals=0
        ),
        name="column_slices",
    )(order, ring, matrix)


def rows_kernel(*refs):
    *parts, out_ref = refs
    start = 0
    for part in parts:
        out_ref[start : start + part.shape[0], :] = part[...]
        start += part.shape[0]


def stacked_rows(*parts):
    rows = sum(part.shape[0] for part in parts)
    vmem = pl.BlockSpec(memory_space=pltpu.VMEM)
    return pl.pallas_call(
        rows_kernel,
        in_specs=[vmem] * len(parts),
        out_specs=vmem,
        out_shape=jax.ShapeDtypeStruct((rows, parts[0].shape[1]), parts[0].dtype),
        cost_estimate=pl.CostEstimate(
            flops=0, bytes_accessed=4 * rows * parts[0].shape[1], transcendentals=0
        ),
        name="stacked_rows",
    )(*parts)


def after(value, earlier):
    return lax.optimization_barrier((value, earlier))[0]


def at_index(array, index, axis=0):
    return lax.dynamic_index_in_dim(array, index, axis=axis, keepdims=False)


def other_core(y, x, core):
    return y, x, 1 - core


def pair(y, x, core):
    return y ^ 1, x, core


def by_two(y, x, core):
    return y ^ 2, x, core


def around(y, x, core):
    return y, (x + 1 - 2 * core) % 4, core


def same(y, x, core):
    return y, x, core


def shards(section_input, norm_gain, qkv_weight, out_weight, random_blocks, global_blocks):
    yl, x, core, seq = (lax.axis_index(axis) for axis in PLANE)
    f32, bf16 = jnp.float32, jnp.bfloat16
    tokens_t = section_input[0].T
    part, length = tokens_t.shape
    step = length // 2
    width = part * 32
    first = yl // 2

    def of_core(array):
        halves = array[:, :step], array[:, step:]
        return jnp.where(core == 0, *halves), jnp.where(core == 0, *halves[::-1])

    own, away = of_core(tokens_t)
    crossed = moved(away, lambda *at: other_core(*swap_inner(*at)))
    e = stacked_rows(moved(own, swap_inner), crossed)
    out_next = moved_on(out_weight[0].T, same)

    gain = norm_gain
    gain_row = jnp.pad(gain, ((0, 15), (0, step - part)))
    beside = moved(jnp.concatenate([away, gain_row], axis=0), other_core)
    gain = jnp.concatenate([gain, beside[part : part + 1, :part]], axis=1).astype(f32)
    item = jnp.concatenate([own, beside[:part]], axis=0)
    as_float = item.astype(f32)
    squares = jnp.sum(as_float * as_float, axis=0)
    random = random_blocks[0]
    numbers = jnp.pad(random.astype(f32).reshape(-1), (0, step - random.size))
    mine = jnp.stack([squares, numbers])
    theirs = moved(mine, other_seq)
    random = jnp.stack([theirs[1, : random.size].astype(jnp.int32).reshape(random.shape), random])
    slot = (yl * 4 + x == jnp.arange(16))[:, None]
    table = jnp.where(slot, jnp.pad(gain, ((0, 0), (0, step - 2 * part))), 0.0)
    table = jnp.concatenate([table, mine[:1], theirs[:1]], axis=0)
    table = table + moved(table, lambda y, x, c: (y, x ^ 1, c))
    weight = after(qkv_weight[0], theirs)
    weight_beside = moved(weight, other_core)
    f = moved(e, by_two)
    e_two = stacked_rows(e, moved(after(e, table), pair))
    f_two = stacked_rows(f, moved(f, pair))
    e_ring, f_ring = [e_two], [f_two]
    for _ in range(3):
        e_ring.append(moved(e_ring[-1], around))
        f_ring.append(moved(f_ring[-1], around))
    table = after(table, e_ring[1])
    for where in (lambda y, x, c: (y, x ^ 2, c), pair, by_two):
        table = table + moved(table, where)
    factors = lax.rsqrt(table[16:] / width + 1e-05)
    factor_e = jnp.where(first == seq, factors[:1], factors[1:])
    factor_f = jnp.where(first == seq, factors[1:], factors[:1])
    gains = table[:16, : 2 * part].reshape(2, 2, 4, 2 * part)
    gains = at_index(gains, seq)

    beside = weight_beside
    columns = weight.shape[1]
    weight = jnp.concatenate(
        [jnp.where(core == seq, weight, beside), jnp.where(core == seq, beside, weight)], axis=1
    )
    weight = weight.reshape(2, 4, 2, part, 2 * columns)
    weights, scales = [], []
    for k in range(4):
        source = (x - (1 - 2 * core) * k) % 4
        rows, scale = [], []
        for ab in range(2):
            which = ab ^ (yl % 2)
            block = at_index(at_index(weight, which), source)
            rows += [at_index(block, core), at_index(block, 1 - core)]
            scale.append(at_index(at_index(gains, which), source))
        weights.append(jnp.concatenate(rows, axis=0).T)
        scales.append(jnp.concatenate(scale).reshape(4 * part, 1))

    def project(block, k, factor):
        normed = (block.astype(f32) * factor * scales[k]).astype(bf16)
        return jnp.dot(weights[k], normed, preferred_element_type=f32)

    count = step // BLOCK
    rows = lax.dynamic_slice_in_dim(random, core * count, count, axis=1).reshape(2 * count, -1)
    spot = jnp.arange(count, dtype=jnp.int32)

    def block_ids(halves, core):
        halves = jnp.stack(halves) * 2 * count
        return (halves[:, None] + core * count + spot[None, :]).reshape(-1)

    query_ids = block_ids([1 - seq, seq], core)
    key_ids = jnp.concatenate(
        [block_ids([first, 1 - first], core), block_ids([first, 1 - first], 1 - core)]
    )
    allowed = block_mask(query_ids, rows, global_blocks[0], key_ids)
    bias = jnp.repeat(jnp.where(allowed.T, 0.0, NEG), BLOCK, axis=1).astype(bf16)

    partial_e = partial_f = 0.0
    for k in range(4):
        partial_e = partial_e + project(e_ring[k], k, factor_e)
        partial_f = partial_f + project(f_ring[k], k, factor_f)
    order = after(jnp.stack([yl, yl ^ 2, yl ^ 1, yl ^ 3]), f_two)
    ring = (x + jnp.arange(4, dtype=jnp.int32)) % 4
    slices = column_slices(out_next, order, ring)
    sends = [partial[columns:].astype(bf16) for partial in (partial_e, partial_f)]
    sends[0], slices = lax.optimization_barrier((sends[0], slices))
    out_own = [slices[0]]
    for r in range(1, 4):
        out_own.append(moved(slices[r], lambda y, x, c, r=r: (y, (x + r) % 4, c)))
    joined, other = [], []
    head = columns // 3
    for partial, send in zip((partial_e, partial_f), sends):
        came = moved(send, other_seq)
        joined.append((partial[:columns] + came.astype(f32)).astype(bf16))
        other.append(moved(joined[-1][head:], other_core))

    flag = after((first == seq).astype(jnp.int32).reshape(1), out_own)
    out_own = stacked_rows(*out_own)
    out_cols = out_own, moved(out_own, other_core)
    sent, kept = attention(flag, joined, other, bias)
    came, kept = moved_on(sent, other_seq), moved_on(kept, same)

    heads = jnp.concatenate(
        [jnp.where(seq == 0, kept, came), jnp.where(seq == 0, came, kept)], axis=0
    )
    far = moved(heads, by_two)
    blocks = [heads, far, moved(heads, pair), moved(far, pair)]
    per = heads.shape[0]
    added = []
    for cols in out_cols:
        total = 0.0
        for p, block in enumerate(blocks):
            total = total + jnp.dot(
                cols[:, p * per : (p + 1) * per], block, preferred_element_type=f32
            )
        added.append(total)
    total = jnp.concatenate([half[:part] for half in added], axis=0)
    shares = []
    for r in range(1, 4):
        share = jnp.concatenate(
            [half[r * part : (r + 1) * part].astype(bf16) for half in added], axis=0
        )
        shares.append(moved(share, lambda y, x, c, r=r: (y, (x - r) % 4, c)))
    residual = moved_on(after(item, shares[0]), same)
    total = residual.astype(f32) + total
    for share in shares:
        total = total + share.astype(f32)
    result = total.astype(bf16)

    own, away = result[:part], moved(result[part:], other_core)
    handed_on = jnp.concatenate(
        [jnp.where(core == 0, own, away), jnp.where(core == 0, away, own)], axis=1
    )
    return handed_on.T[None]


def solution(mesh):
    fine = Mesh(mesh.devices.reshape(8, 4, 4, 2, 2), ("section", "yl", "x", "core", "seq"))
    placed = (
        P("section", "seq", DP),
        P("section", DP),
        P("section", "seq", DP),
        P("section", None, DP),
        P("section", "seq", None),
        P("section", None),
    )
    return jax.shard_map(
        shards, mesh=fine, in_specs=placed, out_specs=P("section", "seq", DP), check_vma=False
    )
```

```python
import math

import jax
import jax.numpy as jnp
from jax import lax
from jax.experimental import pallas as pl
from jax.experimental.pallas import tpu as pltpu
from jax.sharding import Mesh, PartitionSpec as P

BLOCK = 64
PLANE = ("yl", "x", "core", "seq")
DP = ("yl", "x", "core")
NEG = -1e30


def pairs_of(where):
    pairs = []
    for yl in range(4):
        for x in range(4):
            for core in range(2):
                for seq in range(2):
                    target = where(seq * 4 + yl, x, core)
                    if target is None:
                        continue
                    ty, tx, tc = target
                    source_at = ((yl * 4 + x) * 2 + core) * 2 + seq
                    target_at = (((ty % 4) * 4 + tx) * 2 + tc) * 2 + ty // 4
                    pairs.append((source_at, target_at))
    return pairs


def moved(value, where):
    return lax.ppermute(value, PLANE, pairs_of(where))


def moved_on(value, where):
    sections, plane = lax.axis_size("section"), 64
    pairs = [
        (i * plane + a, (i + 1) % sections * plane + b)
        for i in range(sections)
        for a, b in pairs_of(where)
    ]
    return lax.ppermute(value, ("section", *PLANE), pairs)


def swap_inner(y, x, core):
    if y in (2, 3):
        return y + 2, x, core
    if y in (4, 5):
        return y - 2, x, core
    return y, x, core


def other_seq(y, x, core):
    return (y + 4) % 8, x, core


def block_mask(query_ids, random_rows, global_ids, key_ids):
    query_col = query_ids[:, None]
    key_ids = key_ids[None, :]
    adjacent = jnp.abs(query_col - key_ids) <= 1
    key_global = jnp.any(key_ids[:, :, None] == global_ids[None, None, :], axis=2)
    query_global = jnp.any(query_col[:, :, None] == global_ids[None, None, :], axis=2)
    chosen = jnp.any(random_rows[:, None, :] == key_ids[:, :, None], axis=2)
    return adjacent | key_global | query_global | chosen


def attention_kernel(scale, per, flag_ref, *refs):
    own_refs, other_refs = refs[:2], refs[2:4]
    bias_ref, sent_ref, kept_ref, rows_ref, value_ref, wide_ref = refs[4:]
    size, tile = sent_ref.shape
    at = pl.program_id(0)

    @pl.when(at == 0)
    def _():
        step = per * tile
        for i in range(2):
            here, there = pl.ds(i * step, step), pl.ds((2 + i) * step, step)
            rows_ref[here, :size] = own_refs[i][size : 2 * size, :].T
            rows_ref[there, :size] = other_refs[i][:size, :].T
            value_ref[:, here] = own_refs[i][2 * size :, :]
            value_ref[:, there] = other_refs[i][size:, :]
        shape = (rows_ref.shape[0], size)
        block = lax.broadcasted_iota(jnp.int32, shape, 0) // BLOCK
        column = lax.broadcasted_iota(jnp.int32, shape, 1)
        rows_ref[:, size:] = jnp.where(block == column, 1.0, 0.0).astype(jnp.bfloat16)
        wide_ref[...] = jnp.zeros_like(wide_ref)

    columns = pl.ds(pl.multiple_of(lax.rem(at, per) * tile, tile), tile)
    use_f = (at < per) == (flag_ref[0] > 0)

    @pl.when(use_f)
    def _():
        wide_ref[:size, :] = own_refs[1][:size, columns]

    @pl.when(jnp.logical_not(use_f))
    def _():
        wide_ref[:size, :] = own_refs[0][:size, columns]

    wide_ref[size : size + bias_ref.shape[0], :] = bias_ref[...]
    scores = jnp.dot(rows_ref[...], wide_ref[...], preferred_element_type=jnp.float32)
    highest = jnp.max(scores, axis=0, keepdims=True)
    weights = jnp.exp((scores - highest) * scale)
    totals = jnp.sum(weights, axis=0, keepdims=True)
    mixed = jnp.dot(
        value_ref[...], weights.astype(jnp.bfloat16), preferred_element_type=jnp.float32
    )
    mixed = (mixed / totals).astype(jnp.bfloat16)

    @pl.when(at < per)
    def _():
        sent_ref[...] = mixed

    @pl.when(at >= per)
    def _():
        kept_ref[...] = mixed


def attention(flag, own, other, bias):
    triple, step = own[0].shape
    size, tile = triple // 3, 256
    per = step // tile

    def whole(array):
        return pl.BlockSpec(array.shape, lambda i, flag: (0, 0))

    return pl.pallas_call(
        lambda *refs: attention_kernel(1.0 / math.sqrt(size), per, *refs),
        grid_spec=pltpu.PrefetchScalarGridSpec(
            num_scalar_prefetch=1,
            grid=(2 * per,),
            in_specs=[whole(array) for array in (*own, *other)]
            + [pl.BlockSpec((bias.shape[0], tile), lambda i, flag: (0, i))],
            out_specs=[
                pl.BlockSpec((size, tile), lambda i, flag: (0, jnp.minimum(i, per - 1))),
                pl.BlockSpec((size, tile), lambda i, flag: (0, jnp.maximum(i - per, 0))),
            ],
            scratch_shapes=[
                pltpu.VMEM((4 * step, 2 * size), jnp.bfloat16),
                pltpu.VMEM((size, 4 * step), jnp.bfloat16),
                pltpu.VMEM((2 * size, tile), jnp.bfloat16),
            ],
        ),
        out_shape=[jax.ShapeDtypeStruct((size, step), jnp.bfloat16)] * 2,
        cost_estimate=pl.CostEstimate(
            flops=32 * size * step * step, bytes_accessed=12 * size * step, transcendentals=8 * step * step
        ),
        name="attention",
    )(flag, *own, *other, bias)


def slices_kernel(order_ref, ring_ref, source_ref, *out_refs):
    for r, out_ref in enumerate(out_refs):
        per = out_ref.shape[1]
        start = pl.multiple_of(ring_ref[r] * per, per)
        out_ref[...] = source_ref[:, pl.ds(start, per)]


def column_slices(matrix, order, ring):
    rows, width = matrix.shape
    block = pl.BlockSpec((rows, width // 16), lambda p, order, ring: (0, p))
    return pl.pallas_call(
        slices_kernel,
        grid_spec=pltpu.PrefetchScalarGridSpec(
            num_scalar_prefetch=2,
            grid=(4,),
            in_specs=[pl.BlockSpec((rows, width // 4), lambda p, order, ring: (0, order[p]))],
            out_specs=[block] * 4,
        ),
        out_shape=[jax.ShapeDtypeStruct((rows, width // 4), matrix.dtype)] * 4,
        cost_estimate=pl.CostEstimate(
            flops=0, bytes_accessed=4 * rows * width, transcendentals=0
        ),
        name="column_slices",
    )(order, ring, matrix)


def rows_kernel(*refs):
    *parts, out_ref = refs
    start = 0
    for part in parts:
        out_ref[start : start + part.shape[0], :] = part[...]
        start += part.shape[0]


def stacked_rows(*parts):
    rows = sum(part.shape[0] for part in parts)
    vmem = pl.BlockSpec(memory_space=pltpu.VMEM)
    return pl.pallas_call(
        rows_kernel,
        in_specs=[vmem] * len(parts),
        out_specs=vmem,
        out_shape=jax.ShapeDtypeStruct((rows, parts[0].shape[1]), parts[0].dtype),
        cost_estimate=pl.CostEstimate(
            flops=0, bytes_accessed=4 * rows * parts[0].shape[1], transcendentals=0
        ),
        name="stacked_rows",
    )(*parts)


def after(value, earlier):
    return lax.optimization_barrier((value, earlier))[0]


def at_index(array, index, axis=0):
    return lax.dynamic_index_in_dim(array, index, axis=axis, keepdims=False)


def other_core(y, x, core):
    return y, x, 1 - core


def pair(y, x, core):
    return y ^ 1, x, core


def by_two(y, x, core):
    return y ^ 2, x, core


def around(y, x, core):
    return y, (x + 1 - 2 * core) % 4, core


def same(y, x, core):
    return y, x, core


def shards(section_input, norm_gain, qkv_weight, out_weight, random_blocks, global_blocks):
    yl, x, core, seq = (lax.axis_index(axis) for axis in PLANE)
    f32, bf16 = jnp.float32, jnp.bfloat16
    tokens_t = section_input[0].T
    part, length = tokens_t.shape
    step = length // 2
    width = part * 32
    first = yl // 2

    def of_core(array):
        halves = array[:, :step], array[:, step:]
        return jnp.where(core == 0, *halves), jnp.where(core == 0, *halves[::-1])

    own, away = of_core(tokens_t)
    crossed = moved(away, lambda *at: other_core(*swap_inner(*at)))
    e = stacked_rows(moved(own, swap_inner), crossed)
    out_next = moved_on(out_weight[0].T, same)

    gain = norm_gain
    gain_row = jnp.pad(gain, ((0, 15), (0, step - part)))
    beside = moved(jnp.concatenate([away, gain_row], axis=0), other_core)
    gain = jnp.concatenate([gain, beside[part : part + 1, :part]], axis=1).astype(f32)
    item = jnp.concatenate([own, beside[:part]], axis=0)
    as_float = item.astype(f32)
    squares = jnp.sum(as_float * as_float, axis=0)
    random = random_blocks[0]
    numbers = jnp.pad(random.astype(f32).reshape(-1), (0, step - random.size))
    mine = jnp.stack([squares, numbers])
    theirs = moved(mine, other_seq)
    random = jnp.stack([theirs[1, : random.size].astype(jnp.int32).reshape(random.shape), random])
    slot = (yl * 4 + x == jnp.arange(16))[:, None]
    table = jnp.where(slot, jnp.pad(gain, ((0, 0), (0, step - 2 * part))), 0.0)
    table = jnp.concatenate([table, mine[:1], theirs[:1]], axis=0)
    table = table + moved(table, lambda y, x, c: (y, x ^ 1, c))
    weight = after(qkv_weight[0], theirs)
    weight_beside = moved(weight, other_core)
    f = moved(e, by_two)
    e_two = stacked_rows(e, after(moved(after(e, table), pair), f))
    f_two = stacked_rows(f, moved(f, pair))
    e_ring, f_ring = [e_two], [f_two]
    for _ in range(2):
        e_ring.append(moved(e_ring[-1], around))
        f_ring.append(moved(f_ring[-1], around))
    table = after(table, (e_ring[1], f_two))
    for where in (lambda y, x, c: (y, x ^ 2, c), pair):
        table = table + moved(table, where)
    table = after(table, (e_ring[2], f_ring[1]))
    table = table + moved(table, by_two)
    factors = lax.rsqrt(table[16:] / width + 1e-05)
    factor_e = jnp.where(first == seq, factors[:1], factors[1:])
    factor_f = jnp.where(first == seq, factors[1:], factors[:1])
    gains = table[:16, : 2 * part].reshape(2, 2, 4, 2 * part)
    gains = at_index(gains, seq)

    beside = weight_beside
    columns = weight.shape[1]
    weight = jnp.concatenate(
        [jnp.where(core == seq, weight, beside), jnp.where(core == seq, beside, weight)], axis=1
    )
    weight = weight.reshape(2, 4, 2, part, 2 * columns)
    weights, scales = [], []
    for k in range(4):
        source = (x - (1 - 2 * core) * k) % 4
        rows, scale = [], []
        for ab in range(2):
            which = ab ^ (yl % 2)
            block = at_index(at_index(weight, which), source)
            rows += [at_index(block, core), at_index(block, 1 - core)]
            scale.append(at_index(at_index(gains, which), source))
        weights.append(jnp.concatenate(rows, axis=0).T)
        scales.append(jnp.concatenate(scale).reshape(4 * part, 1))

    def project(block, k, factor):
        normed = (block.astype(f32) * factor * scales[k]).astype(bf16)
        return jnp.dot(weights[k], normed, preferred_element_type=f32)

    count = step // BLOCK
    rows = lax.dynamic_slice_in_dim(random, core * count, count, axis=1).reshape(2 * count, -1)
    spot = jnp.arange(count, dtype=jnp.int32)

    def block_ids(halves, core):
        halves = jnp.stack(halves) * 2 * count
        return (halves[:, None] + core * count + spot[None, :]).reshape(-1)

    query_ids = block_ids([1 - seq, seq], core)
    key_ids = jnp.concatenate(
        [block_ids([first, 1 - first], core), block_ids([first, 1 - first], 1 - core)]
    )
    allowed = block_mask(query_ids, rows, global_blocks[0], key_ids)
    bias = jnp.repeat(jnp.where(allowed.T, 0.0, NEG), BLOCK, axis=1).astype(bf16)

    partial_e = project(e_ring[0], 0, factor_e) + project(e_ring[1], 1, factor_e)
    last, partial_e = lax.optimization_barrier((e_ring[2], partial_e))
    partial_e = partial_e + project(last, 2, factor_e)
    e_last = moved(last, around)
    partial_f = project(f_ring[0], 0, factor_f) + project(f_ring[1], 1, factor_f)
    last, partial_e, partial_f = lax.optimization_barrier((f_ring[2], partial_e, partial_f))
    f_last = moved(last, around)
    partial_f = partial_f + project(last, 2, factor_f)
    partial_e = partial_e + project(e_last, 3, factor_e)
    partial_f = partial_f + project(f_last, 3, factor_f)
    order = after(jnp.stack([yl, yl ^ 2, yl ^ 1, yl ^ 3]), f_two)
    ring = (x + jnp.arange(4, dtype=jnp.int32)) % 4
    slices = column_slices(out_next, order, ring)
    sends = [partial[columns:].astype(bf16) for partial in (partial_e, partial_f)]
    sends[0], slices = lax.optimization_barrier((sends[0], slices))
    out_own = [slices[0]]
    for r in range(1, 4):
        out_own.append(moved(slices[r], lambda y, x, c, r=r: (y, (x + r) % 4, c)))
    joined, other = [], []
    head = columns // 3
    residual = moved_on(after(item, sends[1]), same)
    for i, (partial, send) in enumerate(zip((partial_e, partial_f), sends)):
        came = moved(send, other_seq)
        came = after(came, residual) if i else came
        joined.append((partial[:columns] + came.astype(f32)).astype(bf16))
        other.append(moved(joined[-1][head:], other_core))

    flag = after((first == seq).astype(jnp.int32).reshape(1), out_own)
    out_own = stacked_rows(*out_own)
    out_cols = out_own, moved(out_own, other_core)
    sent, kept = attention(flag, joined, other, bias)
    came, kept = moved_on(sent, other_seq), moved_on(kept, same)

    heads = jnp.concatenate(
        [jnp.where(seq == 0, kept, came), jnp.where(seq == 0, came, kept)], axis=0
    )
    far = moved(heads, by_two)
    blocks = [heads, far, moved(heads, pair), moved(far, pair)]
    per = heads.shape[0]
    added = []
    for cols in out_cols:
        total = 0.0
        for p, block in enumerate(blocks):
            total = total + jnp.dot(
                cols[:, p * per : (p + 1) * per], block, preferred_element_type=f32
            )
        added.append(total)
    total = jnp.concatenate([half[:part] for half in added], axis=0)
    shares = []
    for r in range(1, 4):
        share = jnp.concatenate(
            [half[r * part : (r + 1) * part].astype(bf16) for half in added], axis=0
        )
        shares.append(moved(share, lambda y, x, c, r=r: (y, (x - r) % 4, c)))
    total = residual.astype(f32) + total
    for share in shares:
        total = total + share.astype(f32)
    result = total.astype(bf16)

    own, away = result[:part], moved(result[part:], other_core)
    handed_on = jnp.concatenate(
        [jnp.where(core == 0, own, away), jnp.where(core == 0, away, own)], axis=1
    )
    return handed_on.T[None]


def solution(mesh):
    fine = Mesh(mesh.devices.reshape(8, 4, 4, 2, 2), ("section", "yl", "x", "core", "seq"))
    placed = (
        P("section", "seq", DP),
        P("section", DP),
        P("section", "seq", DP),
        P("section", None, DP),
        P("section", "seq", None),
        P("section", None),
    )
    return jax.shard_map(
        shards, mesh=fine, in_specs=placed, out_specs=P("section", "seq", DP), check_vma=False
    )
```

```python
import math

import jax
import jax.numpy as jnp
import numpy as np
from jax import lax
from jax.experimental import pallas as pl
from jax.experimental.pallas import tpu as pltpu
from jax.sharding import Mesh, PartitionSpec as P

BLOCK = 64
PLANE = ("yl", "x", "core", "seq")
DP = ("yl", "x", "core")
NEG = -1e30
TOP = 3.38e38


def pairs_of(where):
    pairs = []
    for yl in range(4):
        for x in range(4):
            for core in range(2):
                for seq in range(2):
                    target = where(seq * 4 + yl, x, core)
                    if target is None:
                        continue
                    ty, tx, tc = target
                    source_at = ((yl * 4 + x) * 2 + core) * 2 + seq
                    target_at = (((ty % 4) * 4 + tx) * 2 + tc) * 2 + ty // 4
                    pairs.append((source_at, target_at))
    return pairs


def moved(value, where):
    return lax.ppermute(value, PLANE, pairs_of(where))


def moved_on(value, where):
    sections, plane = lax.axis_size("section"), 64
    pairs = [
        (i * plane + a, (i + 1) % sections * plane + b)
        for i in range(sections)
        for a, b in pairs_of(where)
    ]
    return lax.ppermute(value, ("section", *PLANE), pairs)


def swap_inner(y, x, core):
    if y in (2, 3):
        return y + 2, x, core
    if y in (4, 5):
        return y - 2, x, core
    return y, x, core


def other_seq(y, x, core):
    return (y + 4) % 8, x, core


def block_mask(query_ids, random_rows, global_ids, key_ids):
    query_col = query_ids[:, None]
    key_ids = key_ids[None, :]
    adjacent = jnp.abs(query_col - key_ids) <= 1
    key_global = jnp.any(key_ids[:, :, None] == global_ids[None, None, :], axis=2)
    query_global = jnp.any(query_col[:, :, None] == global_ids[None, None, :], axis=2)
    chosen = jnp.any(random_rows[:, None, :] == key_ids[:, :, None], axis=2)
    return adjacent | key_global | query_global | chosen


def attention_kernel(scale, per, flag_ref, *refs):
    own_refs, other_refs = refs[:2], refs[2:4]
    bias_ref, sent_ref, kept_ref, rows_ref, value_ref, wide_ref = refs[4:]
    size, tile = sent_ref.shape
    at = pl.program_id(0)

    @pl.when(at == 0)
    def _():
        step = per * tile
        for i in range(2):
            here, there = pl.ds(i * step, step), pl.ds((2 + i) * step, step)
            rows_ref[here, :size] = own_refs[i][size : 2 * size, :].T
            rows_ref[there, :size] = other_refs[i][:size, :].T
            value_ref[:, here] = own_refs[i][2 * size :, :]
            value_ref[:, there] = other_refs[i][size:, :]
        shape = (rows_ref.shape[0], size)
        block = lax.broadcasted_iota(jnp.int32, shape, 0) // BLOCK
        column = lax.broadcasted_iota(jnp.int32, shape, 1)
        rows_ref[:, size:] = jnp.where(block == column, 1.0, 0.0).astype(jnp.bfloat16)
        wide_ref[...] = jnp.zeros_like(wide_ref)

    columns = pl.ds(pl.multiple_of(lax.rem(at, per) * tile, tile), tile)
    use_f = (at < per) == (flag_ref[0] > 0)

    @pl.when(use_f)
    def _():
        wide_ref[:size, :] = own_refs[1][:size, columns]

    @pl.when(jnp.logical_not(use_f))
    def _():
        wide_ref[:size, :] = own_refs[0][:size, columns]

    wide_ref[size : size + bias_ref.shape[0], :] = bias_ref[...]
    scores = jnp.dot(rows_ref[...], wide_ref[...], preferred_element_type=jnp.float32)
    highest = jnp.max(scores, axis=0, keepdims=True)
    weights = jnp.exp((scores - highest) * scale)
    totals = jnp.sum(weights, axis=0, keepdims=True)
    mixed = jnp.dot(
        value_ref[...], weights.astype(jnp.bfloat16), preferred_element_type=jnp.float32
    )
    mixed = (mixed / totals).astype(jnp.bfloat16)

    @pl.when(at < per)
    def _():
        sent_ref[...] = mixed

    @pl.when(at >= per)
    def _():
        kept_ref[...] = mixed


def attention(flag, own, other, bias):
    triple, step = own[0].shape
    size, tile = triple // 3, 256
    per = step // tile

    def whole(array):
        return pl.BlockSpec(array.shape, lambda i, flag: (0, 0))

    return pl.pallas_call(
        lambda *refs: attention_kernel(1.0 / math.sqrt(size), per, *refs),
        grid_spec=pltpu.PrefetchScalarGridSpec(
            num_scalar_prefetch=1,
            grid=(2 * per,),
            in_specs=[whole(array) for array in (*own, *other)]
            + [pl.BlockSpec((bias.shape[0], tile), lambda i, flag: (0, i))],
            out_specs=[
                pl.BlockSpec((size, tile), lambda i, flag: (0, jnp.minimum(i, per - 1))),
                pl.BlockSpec((size, tile), lambda i, flag: (0, jnp.maximum(i - per, 0))),
            ],
            scratch_shapes=[
                pltpu.VMEM((4 * step, 2 * size), jnp.bfloat16),
                pltpu.VMEM((size, 4 * step), jnp.bfloat16),
                pltpu.VMEM((2 * size, tile), jnp.bfloat16),
            ],
        ),
        out_shape=[jax.ShapeDtypeStruct((size, step), jnp.bfloat16)] * 2,
        cost_estimate=pl.CostEstimate(
            flops=32 * size * step * step, bytes_accessed=12 * size * step, transcendentals=8 * step * step
        ),
        name="attention",
    )(flag, *own, *other, bias)


def slices_kernel(order_ref, ring_ref, source_ref, *out_refs):
    for r, out_ref in enumerate(out_refs):
        per = out_ref.shape[1]
        start = pl.multiple_of(ring_ref[r] * per, per)
        out_ref[...] = source_ref[:, pl.ds(start, per)]


def column_slices(matrix, order, ring):
    rows, width = matrix.shape
    block = pl.BlockSpec((rows, width // 16), lambda p, order, ring: (0, p))
    return pl.pallas_call(
        slices_kernel,
        grid_spec=pltpu.PrefetchScalarGridSpec(
            num_scalar_prefetch=2,
            grid=(4,),
            in_specs=[pl.BlockSpec((rows, width // 4), lambda p, order, ring: (0, order[p]))],
            out_specs=[block] * 4,
        ),
        out_shape=[jax.ShapeDtypeStruct((rows, width // 4), matrix.dtype)] * 4,
        cost_estimate=pl.CostEstimate(
            flops=0, bytes_accessed=4 * rows * width, transcendentals=0
        ),
        name="column_slices",
    )(order, ring, matrix)


def rows_kernel(*refs):
    *parts, out_ref = refs
    start = 0
    for part in parts:
        out_ref[start : start + part.shape[0], :] = part[...]
        start += part.shape[0]


def stacked_rows(*parts):
    rows = sum(part.shape[0] for part in parts)
    vmem = pl.BlockSpec(memory_space=pltpu.VMEM)
    return pl.pallas_call(
        rows_kernel,
        in_specs=[vmem] * len(parts),
        out_specs=vmem,
        out_shape=jax.ShapeDtypeStruct((rows, parts[0].shape[1]), parts[0].dtype),
        cost_estimate=pl.CostEstimate(
            flops=0, bytes_accessed=4 * rows * parts[0].shape[1], transcendentals=0
        ),
        name="stacked_rows",
    )(*parts)


def after(value, earlier):
    return lax.optimization_barrier((value, earlier))[0]


def at_index(array, index, axis=0):
    return lax.dynamic_index_in_dim(array, index, axis=axis, keepdims=False)


def other_core(y, x, core):
    return y, x, 1 - core


def pair(y, x, core):
    return y ^ 1, x, core


def by_two(y, x, core):
    return y ^ 2, x, core


def around(y, x, core):
    return y, (x + 1 - 2 * core) % 4, core


def three_rows(values):
    values = jnp.minimum(values, TOP)
    high = lax.reduce_precision(values, 8, 7)
    middle = lax.reduce_precision(values - high, 8, 7)
    rows = [high, middle, values - high - middle]
    rows = jnp.concatenate([row.astype(jnp.bfloat16) for row in rows], axis=0)
    return jnp.pad(rows, ((0, 13), (0, 0)))


def same(y, x, core):
    return y, x, core


def shards(section_input, norm_gain, qkv_weight, out_weight, random_blocks, global_blocks):
    yl, x, core, seq = (lax.axis_index(axis) for axis in PLANE)
    f32, bf16 = jnp.float32, jnp.bfloat16
    tokens_t = section_input[0].T
    part, length = tokens_t.shape
    step = length // 2
    width = part * 32
    first = yl // 2

    def of_core(array):
        halves = array[:, :step], array[:, step:]
        return jnp.where(core == 0, *halves), jnp.where(core == 0, *halves[::-1])

    as_float = tokens_t.astype(f32)
    gained = jnp.clip(as_float * norm_gain.astype(f32).T, -TOP, TOP).astype(bf16)
    squares = jnp.sum(as_float * as_float, axis=0, keepdims=True)
    own, away = of_core(jnp.concatenate([gained, three_rows(squares)], axis=0))
    crossed = moved(away, lambda *at: other_core(*swap_inner(*at)))
    e = stacked_rows(moved(own, swap_inner), crossed)
    random = random_blocks[0]
    random = jnp.stack([moved(random, other_seq), random])
    f = moved(e, by_two)
    e_two = stacked_rows(e, moved(after(e, random), pair))
    f_two = stacked_rows(f, moved(f, pair))

    out_next = moved_on(out_weight[0].T, same)

    own, away = of_core(tokens_t)
    beside = moved(away, other_core)
    item = jnp.concatenate([own, beside], axis=0)
    residual = moved_on(item, same)

    weight = after(qkv_weight[0], beside)
    beside = moved(weight, other_core)
    columns = weight.shape[1]
    weight = jnp.concatenate(
        [jnp.where(core == seq, weight, beside), jnp.where(core == seq, beside, weight)], axis=1
    )
    weight = weight.reshape(16, part, 2 * columns)
    adding = np.zeros((1, part + 16, 2 * columns + 128), np.float32)
    adding[0, part : part + 3, 2 * columns] = 1.0
    weight = jnp.pad(weight, ((0, 0), (0, 16), (0, 128))) + jnp.asarray(adding, bf16)
    weight = weight.reshape(2, 4, 2, part + 16, 2 * columns + 128)
    weights = []
    for k in range(4):
        source = (x - (1 - 2 * core) * k) % 4
        rows = []
        for ab in range(2):
            block = at_index(at_index(weight, ab ^ (yl % 2)), source)
            rows += [at_index(block, core), at_index(block, 1 - core)]
        weights.append(jnp.concatenate(rows, axis=0))

    def project(block, k):
        return lax.dot_general(
            weights[k], block, (((0,), (0,)), ((), ())), preferred_element_type=f32
        )

    count = step // BLOCK
    rows = lax.dynamic_slice_in_dim(random, core * count, count, axis=1).reshape(2 * count, -1)
    spot = jnp.arange(count, dtype=jnp.int32)

    def block_ids(halves, core):
        halves = jnp.stack(halves) * 2 * count
        return (halves[:, None] + core * count + spot[None, :]).reshape(-1)

    query_ids = block_ids([1 - seq, seq], core)
    key_ids = jnp.concatenate(
        [block_ids([first, 1 - first], core), block_ids([first, 1 - first], 1 - core)]
    )
    allowed = block_mask(query_ids, rows, global_blocks[0], key_ids)
    bias = jnp.repeat(jnp.where(allowed.T, 0.0, NEG), BLOCK, axis=1).astype(bf16)

    e, f = e_two, f_two
    partial_e, partial_f = project(e, 0), project(f, 0)
    for k in range(1, 4):
        e, f = moved(e, around), moved(f, around)
        partial_e = partial_e + project(e, k)
        partial_f = partial_f + project(f, k)
    order = after(jnp.stack([yl, yl ^ 2, yl ^ 1, yl ^ 3]), f_two)
    ring = (x + jnp.arange(4, dtype=jnp.int32)) % 4
    slices = column_slices(out_next, order, ring)
    sends = [
        jnp.concatenate(
            [
                partial[columns : 2 * columns].astype(bf16),
                three_rows(partial[2 * columns : 2 * columns + 1]),
            ],
            axis=0,
        )
        for partial in (partial_e, partial_f)
    ]
    sends[0], slices = lax.optimization_barrier((sends[0], slices))
    out_own = [slices[0]]
    for r in range(1, 4):
        out_own.append(moved(slices[r], lambda y, x, c, r=r: (y, (x + r) % 4, c)))
    joined, other = [], []
    head = columns // 3
    for partial, send in zip((partial_e, partial_f), sends):
        came = moved(send, other_seq)
        came = after(came, sends[1]).astype(f32)
        squares = partial[2 * columns : 2 * columns + 1]
        squares = squares + jnp.sum(came[columns : columns + 3], axis=0, keepdims=True)
        factor = jnp.where(squares < TOP, lax.rsqrt(squares / width + 1e-05), 0.0)
        normed = (partial[:columns] + came[:columns]) * factor
        joined.append(jnp.where(factor > 0, normed, 0.0).astype(bf16))
        other.append(moved(joined[-1][head:], other_core))

    flag = after((first == seq).astype(jnp.int32).reshape(1), (out_own, residual))
    out_own = stacked_rows(*out_own)
    out_cols = out_own, moved(out_own, other_core)
    sent, kept = attention(flag, joined, other, bias)
    came, kept = moved_on(sent, other_seq), moved_on(kept, same)

    heads = jnp.concatenate(
        [jnp.where(seq == 0, kept, came), jnp.where(seq == 0, came, kept)], axis=0
    )
    far = moved(heads, by_two)
    blocks = [heads, far, moved(heads, pair), moved(far, pair)]
    per = heads.shape[0]
    added = []
    for cols in out_cols:
        total = 0.0
        for p, block in enumerate(blocks):
            total = total + jnp.dot(
                cols[:, p * per : (p + 1) * per], block, preferred_element_type=f32
            )
        added.append(total)
    total = residual.astype(f32) + jnp.concatenate([half[:part] for half in added], axis=0)
    for r in range(1, 4):
        share = jnp.concatenate(
            [half[r * part : (r + 1) * part].astype(bf16) for half in added], axis=0
        )
        total = total + moved(share, lambda y, x, c, r=r: (y, (x - r) % 4, c)).astype(f32)
    result = total.astype(bf16)

    own, away = result[:part], moved(result[part:], other_core)
    handed_on = jnp.concatenate(
        [jnp.where(core == 0, own, away), jnp.where(core == 0, away, own)], axis=1
    )
    return handed_on.T[None]


def solution(mesh):
    fine = Mesh(mesh.devices.reshape(8, 4, 4, 2, 2), ("section", "yl", "x", "core", "seq"))
    placed = (
        P("section", "seq", DP),
        P("section", DP),
        P("section", "seq", DP),
        P("section", None, DP),
        P("section", "seq", None),
        P("section", None),
    )
    return jax.shard_map(
        shards, mesh=fine, in_specs=placed, out_specs=P("section", "seq", DP), check_vma=False
    )
```

```python
import math

import jax
import jax.numpy as jnp
import numpy as np
from jax import lax
from jax.experimental import pallas as pl
from jax.experimental.pallas import tpu as pltpu
from jax.sharding import Mesh, PartitionSpec as P

BLOCK = 64
PLANE = ("yl", "x", "core", "seq")
DP = ("yl", "x", "core")
NEG = -1e30
TOP = 3.38e38


def pairs_of(where):
    pairs = []
    for yl in range(4):
        for x in range(4):
            for core in range(2):
                for seq in range(2):
                    target = where(seq * 4 + yl, x, core)
                    if target is None:
                        continue
                    ty, tx, tc = target
                    source_at = ((yl * 4 + x) * 2 + core) * 2 + seq
                    target_at = (((ty % 4) * 4 + tx) * 2 + tc) * 2 + ty // 4
                    pairs.append((source_at, target_at))
    return pairs


def moved(value, where):
    return lax.ppermute(value, PLANE, pairs_of(where))


def moved_on(value, where):
    sections, plane = lax.axis_size("section"), 64
    pairs = [
        (i * plane + a, (i + 1) % sections * plane + b)
        for i in range(sections)
        for a, b in pairs_of(where)
    ]
    return lax.ppermute(value, ("section", *PLANE), pairs)


def swap_inner(y, x, core):
    if y in (2, 3):
        return y + 2, x, core
    if y in (4, 5):
        return y - 2, x, core
    return y, x, core


def other_seq(y, x, core):
    return (y + 4) % 8, x, core


def block_mask(query_ids, random_rows, global_ids, key_ids):
    query_col = query_ids[:, None]
    key_ids = key_ids[None, :]
    adjacent = jnp.abs(query_col - key_ids) <= 1
    key_global = jnp.any(key_ids[:, :, None] == global_ids[None, None, :], axis=2)
    query_global = jnp.any(query_col[:, :, None] == global_ids[None, None, :], axis=2)
    chosen = jnp.any(random_rows[:, None, :] == key_ids[:, :, None], axis=2)
    return adjacent | key_global | query_global | chosen


def attention_kernel(scale, per, flag_ref, *refs):
    own_refs, other_refs = refs[:2], refs[2:4]
    bias_ref, sent_ref, kept_ref, rows_ref, value_ref, wide_ref = refs[4:]
    size, tile = sent_ref.shape
    at = pl.program_id(0)

    @pl.when(at == 0)
    def _():
        step = per * tile
        for i in range(2):
            here, there = pl.ds(i * step, step), pl.ds((2 + i) * step, step)
            rows_ref[here, :size] = own_refs[i][size : 2 * size, :].T
            rows_ref[there, :size] = other_refs[i][:size, :].T
            value_ref[:, here] = own_refs[i][2 * size :, :]
            value_ref[:, there] = other_refs[i][size:, :]
        shape = (rows_ref.shape[0], size)
        block = lax.broadcasted_iota(jnp.int32, shape, 0) // BLOCK
        column = lax.broadcasted_iota(jnp.int32, shape, 1)
        rows_ref[:, size:] = jnp.where(block == column, 1.0, 0.0).astype(jnp.bfloat16)
        wide_ref[...] = jnp.zeros_like(wide_ref)

    columns = pl.ds(pl.multiple_of(lax.rem(at, per) * tile, tile), tile)
    use_f = (at < per) == (flag_ref[0] > 0)

    @pl.when(use_f)
    def _():
        wide_ref[:size, :] = own_refs[1][:size, columns]

    @pl.when(jnp.logical_not(use_f))
    def _():
        wide_ref[:size, :] = own_refs[0][:size, columns]

    wide_ref[size : size + bias_ref.shape[0], :] = bias_ref[...]
    scores = jnp.dot(rows_ref[...], wide_ref[...], preferred_element_type=jnp.float32)
    highest = jnp.max(scores, axis=0, keepdims=True)
    weights = jnp.exp((scores - highest) * scale)
    totals = jnp.sum(weights, axis=0, keepdims=True)
    mixed = jnp.dot(
        value_ref[...], weights.astype(jnp.bfloat16), preferred_element_type=jnp.float32
    )
    mixed = (mixed / totals).astype(jnp.bfloat16)

    @pl.when(at < per)
    def _():
        sent_ref[...] = mixed

    @pl.when(at >= per)
    def _():
        kept_ref[...] = mixed


def attention(flag, own, other, bias):
    triple, step = own[0].shape
    size, tile = triple // 3, 256
    per = step // tile

    def whole(array):
        return pl.BlockSpec(array.shape, lambda i, flag: (0, 0))

    return pl.pallas_call(
        lambda *refs: attention_kernel(1.0 / math.sqrt(size), per, *refs),
        grid_spec=pltpu.PrefetchScalarGridSpec(
            num_scalar_prefetch=1,
            grid=(2 * per,),
            in_specs=[whole(array) for array in (*own, *other)]
            + [pl.BlockSpec((bias.shape[0], tile), lambda i, flag: (0, i))],
            out_specs=[
                pl.BlockSpec((size, tile), lambda i, flag: (0, jnp.minimum(i, per - 1))),
                pl.BlockSpec((size, tile), lambda i, flag: (0, jnp.maximum(i - per, 0))),
            ],
            scratch_shapes=[
                pltpu.VMEM((4 * step, 2 * size), jnp.bfloat16),
                pltpu.VMEM((size, 4 * step), jnp.bfloat16),
                pltpu.VMEM((2 * size, tile), jnp.bfloat16),
            ],
        ),
        out_shape=[jax.ShapeDtypeStruct((size, step), jnp.bfloat16)] * 2,
        cost_estimate=pl.CostEstimate(
            flops=32 * size * step * step, bytes_accessed=12 * size * step, transcendentals=8 * step * step
        ),
        name="attention",
    )(flag, *own, *other, bias)


def slices_kernel(order_ref, ring_ref, source_ref, *out_refs):
    for r, out_ref in enumerate(out_refs):
        per = out_ref.shape[1]
        start = pl.multiple_of(ring_ref[r] * per, per)
        out_ref[...] = source_ref[:, pl.ds(start, per)]


def column_slices(matrix, order, ring):
    rows, width = matrix.shape
    block = pl.BlockSpec((rows, width // 16), lambda p, order, ring: (0, p))
    return pl.pallas_call(
        slices_kernel,
        grid_spec=pltpu.PrefetchScalarGridSpec(
            num_scalar_prefetch=2,
            grid=(4,),
            in_specs=[pl.BlockSpec((rows, width // 4), lambda p, order, ring: (0, order[p]))],
            out_specs=[block] * 4,
        ),
        out_shape=[jax.ShapeDtypeStruct((rows, width // 4), matrix.dtype)] * 4,
        cost_estimate=pl.CostEstimate(
            flops=0, bytes_accessed=4 * rows * width, transcendentals=0
        ),
        name="column_slices",
    )(order, ring, matrix)


def rows_kernel(*refs):
    *parts, out_ref = refs
    start = 0
    for part in parts:
        out_ref[start : start + part.shape[0], :] = part[...]
        start += part.shape[0]


def stacked_rows(*parts):
    rows = sum(part.shape[0] for part in parts)
    vmem = pl.BlockSpec(memory_space=pltpu.VMEM)
    return pl.pallas_call(
        rows_kernel,
        in_specs=[vmem] * len(parts),
        out_specs=vmem,
        out_shape=jax.ShapeDtypeStruct((rows, parts[0].shape[1]), parts[0].dtype),
        cost_estimate=pl.CostEstimate(
            flops=0, bytes_accessed=4 * rows * parts[0].shape[1], transcendentals=0
        ),
        name="stacked_rows",
    )(*parts)


def after(value, earlier):
    return lax.optimization_barrier((value, earlier))[0]


def at_index(array, index, axis=0):
    return lax.dynamic_index_in_dim(array, index, axis=axis, keepdims=False)


def other_core(y, x, core):
    return y, x, 1 - core


def pair(y, x, core):
    return y ^ 1, x, core


def by_two(y, x, core):
    return y ^ 2, x, core


def around(y, x, core):
    return y, (x + 1 - 2 * core) % 4, core


def three_rows(values):
    values = jnp.minimum(values, TOP)
    high = lax.reduce_precision(values, 8, 7)
    middle = lax.reduce_precision(values - high, 8, 7)
    rows = [high, middle, values - high - middle]
    rows = jnp.concatenate([row.astype(jnp.bfloat16) for row in rows], axis=0)
    return jnp.pad(rows, ((0, 13), (0, 0)))


def same(y, x, core):
    return y, x, core


def shards(section_input, norm_gain, qkv_weight, out_weight, random_blocks, global_blocks):
    yl, x, core, seq = (lax.axis_index(axis) for axis in PLANE)
    f32, bf16 = jnp.float32, jnp.bfloat16
    tokens_t = section_input[0].T
    part, length = tokens_t.shape
    step = length // 2
    width = part * 32
    first = yl // 2

    def of_core(array):
        halves = array[:, :step], array[:, step:]
        return jnp.where(core == 0, *halves), jnp.where(core == 0, *halves[::-1])

    as_float = tokens_t.astype(f32)
    gained = jnp.clip(as_float * norm_gain.astype(f32).T, -TOP, TOP).astype(bf16)
    squares = jnp.sum(as_float * as_float, axis=0, keepdims=True)
    own, away = of_core(jnp.concatenate([gained, three_rows(squares)], axis=0))
    crossed = moved(away, lambda *at: other_core(*swap_inner(*at)))
    e = stacked_rows(moved(own, swap_inner), crossed)
    f = moved(e, by_two)
    e_two = stacked_rows(e, moved(e, pair))
    f_two = stacked_rows(f, moved(f, pair))
    random = random_blocks[0]
    random = jnp.stack([moved(after(random, f_two), other_seq), random])

    out_next = moved_on(out_weight[0].T, same)

    own, away = of_core(tokens_t)
    beside = moved(away, other_core)
    item = jnp.concatenate([own, beside], axis=0)
    residual = moved_on(item, same)

    weight = after(qkv_weight[0], beside)
    beside = moved(weight, other_core)
    columns = weight.shape[1]
    weight = jnp.concatenate(
        [jnp.where(core == seq, weight, beside), jnp.where(core == seq, beside, weight)], axis=1
    )
    weight = weight.reshape(16, part, 2 * columns)
    adding = np.zeros((1, part + 16, 2 * columns + 128), np.float32)
    adding[0, part : part + 3, 2 * columns] = 1.0
    weight = jnp.pad(weight, ((0, 0), (0, 16), (0, 128))) + jnp.asarray(adding, bf16)
    weight = weight.reshape(2, 4, 2, part + 16, 2 * columns + 128)
    weights = []
    for k in range(4):
        source = (x - (1 - 2 * core) * k) % 4
        rows = []
        for ab in range(2):
            block = at_index(at_index(weight, ab ^ (yl % 2)), source)
            rows += [at_index(block, core), at_index(block, 1 - core)]
        weights.append(jnp.concatenate(rows, axis=0))

    def project(block, k):
        return lax.dot_general(
            weights[k], block, (((0,), (0,)), ((), ())), preferred_element_type=f32
        )

    count = step // BLOCK
    rows = lax.dynamic_slice_in_dim(random, core * count, count, axis=1).reshape(2 * count, -1)
    spot = jnp.arange(count, dtype=jnp.int32)

    def block_ids(halves, core):
        halves = jnp.stack(halves) * 2 * count
        return (halves[:, None] + core * count + spot[None, :]).reshape(-1)

    query_ids = block_ids([1 - seq, seq], core)
    key_ids = jnp.concatenate(
        [block_ids([first, 1 - first], core), block_ids([first, 1 - first], 1 - core)]
    )
    allowed = block_mask(query_ids, rows, global_blocks[0], key_ids)
    bias = jnp.repeat(jnp.where(allowed.T, 0.0, NEG), BLOCK, axis=1).astype(bf16)

    e, f = e_two, f_two
    partial_e, partial_f = project(e, 0), project(f, 0)
    for k in range(1, 4):
        e, f = moved(e, around), moved(f, around)
        partial_e = partial_e + project(e, k)
        partial_f = partial_f + project(f, k)
    order = after(jnp.stack([yl, yl ^ 2, yl ^ 1, yl ^ 3]), f_two)
    ring = (x + jnp.arange(4, dtype=jnp.int32)) % 4
    slices = column_slices(out_next, order, ring)
    sends = [
        jnp.concatenate(
            [
                partial[columns : 2 * columns].astype(bf16),
                three_rows(partial[2 * columns : 2 * columns + 1]),
            ],
            axis=0,
        )
        for partial in (partial_e, partial_f)
    ]
    sends[1], slices = lax.optimization_barrier((sends[1], slices))
    out_own = [slices[0]]
    for r in range(1, 4):
        out_own.append(moved(slices[r], lambda y, x, c, r=r: (y, (x + r) % 4, c)))
    joined, other = [], []
    head = columns // 3
    for partial, send in zip((partial_e, partial_f), sends):
        came = moved(send, other_seq)
        came = came.astype(f32)
        squares = partial[2 * columns : 2 * columns + 1]
        squares = squares + jnp.sum(came[columns : columns + 3], axis=0, keepdims=True)
        factor = jnp.where(squares < TOP, lax.rsqrt(squares / width + 1e-05), 0.0)
        normed = (partial[:columns] + came[:columns]) * factor
        joined.append(jnp.where(factor > 0, normed, 0.0).astype(bf16))
        other.append(moved(joined[-1][head:], other_core))

    flag = after((first == seq).astype(jnp.int32).reshape(1), (out_own, residual))
    out_own = stacked_rows(*out_own)
    out_cols = out_own, moved(out_own, other_core)
    sent, kept = attention(flag, joined, other, bias)
    came, kept = moved_on(sent, other_seq), moved_on(kept, same)

    heads = jnp.concatenate(
        [jnp.where(seq == 0, kept, came), jnp.where(seq == 0, came, kept)], axis=0
    )
    far = moved(heads, by_two)
    blocks = [heads, far, moved(heads, pair), moved(far, pair)]
    per = heads.shape[0]
    added = []
    for cols in out_cols:
        total = 0.0
        for p, block in enumerate(blocks):
            total = total + jnp.dot(
                cols[:, p * per : (p + 1) * per], block, preferred_element_type=f32
            )
        added.append(total)
    total = residual.astype(f32) + jnp.concatenate([half[:part] for half in added], axis=0)
    for r in range(1, 4):
        share = jnp.concatenate(
            [half[r * part : (r + 1) * part].astype(bf16) for half in added], axis=0
        )
        total = total + moved(share, lambda y, x, c, r=r: (y, (x - r) % 4, c)).astype(f32)
    result = total.astype(bf16)

    own, away = result[:part], moved(result[part:], other_core)
    handed_on = jnp.concatenate(
        [jnp.where(core == 0, own, away), jnp.where(core == 0, away, own)], axis=1
    )
    return handed_on.T[None]


def solution(mesh):
    fine = Mesh(mesh.devices.reshape(8, 4, 4, 2, 2), ("section", "yl", "x", "core", "seq"))
    placed = (
        P("section", "seq", DP),
        P("section", DP),
        P("section", "seq", DP),
        P("section", None, DP),
        P("section", "seq", None),
        P("section", None),
    )
    return jax.shard_map(
        shards, mesh=fine, in_specs=placed, out_specs=P("section", "seq", DP), check_vma=False
    )
```
